128 devices in a mesh: head: 4 (over x_lo, core), batch: 32 (over y, z, x_hi).
Axes of the slice: x: 4 (x_hi: 2, x_lo: 2; x = x_hi * 2 + x_lo), y: 4, z: 4, core: 2. Of those that a mesh axis runs over, the one named last changes fastest.
Arguments:
- embedded: bfloat16 [4, 512, 2048], P(None, 'batch'), may hold values from -6 to 6
- states: bfloat16 [512, 32, 128, 128], P('batch', 'head'), may hold values from -6 to 6
- w_query: bfloat16 [2048, 2048], P(None, 'head'), may hold values from -0.125 to 0.125
- w_key: bfloat16 [2048, 2048], P(None, 'head'), may hold values from -0.125 to 0.125
- w_value: bfloat16 [2048, 4096], P(None, 'head'), may hold values from -0.125 to 0.125
- w_output_gate: bfloat16 [2048, 4096], P(None, 'head'), may hold values from -0.125 to 0.125
- w_beta: bfloat16 [2048, 32], P(None, 'head'), may hold values from -0.125 to 0.125
- w_decay: bfloat16 [2048, 32], P(None, 'head'), may hold values from -0.125 to 0.125
- decay_rate: float32 [32], replicated, may hold values from 0.05 to 4
- decay_bias: float32 [32], replicated, may hold values from -3 to 1
- head_gain: float32 [128], replicated, may hold values from 0.5 to 1.5
- input_gain: float32 [2048], replicated, may hold values from 0.5 to 1.5
- w_out: bfloat16 [4096, 2048], P('head'), may hold values from -0.09375 to 0.09375
- final_gain: float32 [2048], replicated, may hold values from 0.5 to 1.5
- lm_head: bfloat16 [2048, 131072], P(None, ('head', 'batch')), may hold values from -1 to 1
- targets: int32 [512, 4], replicated, may hold values from 0 to 131071
- active: int32 [512, 4], replicated, may hold values 0 or 1
Outputs:
- scores: float32 [512, 4], P('batch')
The draws below stay inside these ranges and needn't reach their ends.
All inputs are finite; a program needn't handle non-finite values.
Results may differ from the reference program's by a relative error of at most 0.0022.
Values may be sent and summed in bfloat16 or wider, within the bound.
No kernel may reach another device: no remote copies, remote signals or barrier semaphores. Data moves between devices by JAX's collectives and lax.ppermute only.
A program may use at most 128 MiB of HBM per device.

```python
import math
import jax
import jax.numpy as jnp
from jax import lax

D = 2048
HEADS = 32
KEYHEADS = 16
DK = 128
DV = 128
VOCAB = 131072
STEPS = 4
BATCH = 512


def place_ends(result, stream_key, smallest, top_value):
    shape = result.shape
    place = [jax.random.randint(jax.random.fold_in(stream_key, axis), (), 0, shape[axis]) for axis in range(len(shape))]
    result = result.at[tuple(place)].set(smallest)
    longest = shape.index(max(shape))
    place[longest] = (place[longest] + 1) % shape[longest]
    return result.at[tuple(place)].set(top_value)


def shard_levels(own_key, shape, cuts, least, top_value):
    level, own = 1.0, jax.random.fold_in(own_key, 6)
    for axis_at, parts in cuts:
        draws = jnp.exp(jax.random.uniform(jax.random.fold_in(own, axis_at), (parts,), jnp.float32, least / len(cuts), top_value / len(cuts)))
        level = level * jnp.repeat(draws, shape[axis_at] // parts).reshape([-1 if axis == axis_at else 1 for axis in range(len(shape))])
    return level


def bell_draw(key, dims, spread, limit, split=(), kind=jnp.bfloat16):
    drawn = jax.random.normal(key, dims, jnp.float32) * spread
    if len(split) > 0:
        drawn = shard_levels(key, dims, split, -0.22, 0.18) * drawn
    return jnp.clip(drawn, min=-limit, max=limit).astype(kind)


def setup_inputs(seed: int = 0) -> dict:
    streams_of = jax.random.split(jax.random.key(seed), 18)
    return {
        "embedded": bell_draw(streams_of[0], (STEPS, BATCH, D), 1.0, 6.0, ((1, 32),)),
        "states": bell_draw(streams_of[1], (BATCH, HEADS, DK, DV), 0.5, 6.0, ((0, 32), (1, 4))),
        "w_query": bell_draw(streams_of[2], (D, KEYHEADS * DK), D ** -0.5, 0.125, ((1, 4),)),
        "w_key": bell_draw(streams_of[3], (D, KEYHEADS * DK), D ** -0.5, 0.125, ((1, 4),)),
        "w_value": bell_draw(streams_of[4], (D, HEADS * DV), D ** -0.5, 0.125, ((1, 4),)),
        "w_output_gate": bell_draw(streams_of[5], (D, HEADS * DV), D ** -0.5, 0.125, ((1, 4),)),
        "w_beta": bell_draw(streams_of[6], (D, HEADS), D ** -0.5, 0.125, ((1, 4),)),
        "w_decay": bell_draw(streams_of[7], (D, HEADS), D ** -0.5, 0.125, ((1, 4),)),
        "decay_rate": jnp.clip(jnp.exp(jax.random.uniform(streams_of[8], (HEADS,), jnp.float32, math.log(0.05), math.log(4.0))), 0.05, 4.0),
        "decay_bias": jnp.clip(jax.random.uniform(streams_of[9], (HEADS,), jnp.float32, -3.0, 1.0), -3.0, 1.0),
        "head_gain": jnp.clip(1.0 + 0.1 * jax.random.normal(streams_of[10], (DV,), jnp.float32), 0.5, 1.5),
        "input_gain": jnp.clip(1.0 + 0.1 * jax.random.normal(streams_of[11], (D,), jnp.float32), 0.5, 1.5),
        "w_out": bell_draw(streams_of[12], (HEADS * DV, D), (HEADS * DV) ** -0.5, 0.09375, ((0, 4),)),
        "final_gain": jnp.clip(1.0 + 0.1 * jax.random.normal(streams_of[13], (D,), jnp.float32), 0.5, 1.5),
        "lm_head": bell_draw(streams_of[14], (D, VOCAB), 0.066, 1.0, ((1, 128),)),
        "targets": place_ends(jax.random.randint(streams_of[15], (BATCH, STEPS), 0, VOCAB), jax.random.fold_in(streams_of[15], 1), 0, VOCAB - 1).astype(jnp.int32),
        "active": place_ends((jax.random.randint(streams_of[16], (BATCH, STEPS), 0, 4) < 3).astype(jnp.int32), jax.random.fold_in(streams_of[16], 1), 0, 1),
    }


EPS = 1e-06

def rms_scale(values, gain):
    values = values.astype(jnp.float32)
    return values * lax.rsqrt(lax.optimization_barrier(jnp.mean(values * values, axis=-1, keepdims=True)) + EPS) * gain.astype(jnp.float32)

def unit_rows(values):
    return values * lax.rsqrt(lax.optimization_barrier(jnp.sum(values * values, axis=-1, keepdims=True)) + EPS)

def gated_rms_norm(state_readout, gate, head_gain):
    normed = state_readout * lax.rsqrt(lax.optimization_barrier(jnp.mean(state_readout * state_readout, axis=-1, keepdims=True)) + EPS) * head_gain.astype(jnp.float32)
    gate_f = gate.astype(jnp.float32).reshape(state_readout.shape)
    return (normed * jax.nn.silu(gate_f)).astype(jnp.bfloat16)

def one_request(item):
    state, queries, keys, values, betas, decays, marks = item
    state = state.astype(jnp.float32)

    def advance(state, inputs):
        query_vector, key, value, beta, decay, mark = inputs
        decayed_state = state * decay[:, None, None]
        retrieved_value = jnp.einsum('eg,egr->er', key, decayed_state, precision=lax.Precision.HIGHEST)
        update = beta[:, None] * (value - retrieved_value)
        corrected_state = decayed_state + key[:, :, None] * update[:, None, :]
        state_readout = jnp.einsum('eg,egr->er', query_vector, corrected_state, precision=lax.Precision.HIGHEST)
        kept = jnp.where(mark > 0, corrected_state, state)
        return (kept, state_readout)
    _, outs = lax.scan(advance, state, (queries, keys, values, betas, decays, marks))
    return outs

def reference(embedded, states, w_query, w_key, w_value, w_output_gate, w_beta, w_decay, decay_rate, decay_bias, head_gain, input_gain, w_out, final_gain, lm_head, targets, active):
    steps, batch, width = embedded.shape
    normed = rms_scale(embedded, input_gain).astype(jnp.bfloat16).reshape(steps * batch, width)

    def apply_projection(weight):
        return jnp.dot(normed, weight, preferred_element_type=jnp.float32).astype(jnp.bfloat16).reshape(steps, batch, -1)
    query_vector = apply_projection(w_query).astype(jnp.float32).reshape(steps, batch, KEYHEADS, DK)
    key = apply_projection(w_key).astype(jnp.float32).reshape(steps, batch, KEYHEADS, DK)
    value = apply_projection(w_value).astype(jnp.float32).reshape(steps, batch, HEADS, DV)
    gate = apply_projection(w_output_gate)
    beta_raw = apply_projection(w_beta).astype(jnp.float32)
    decay_raw = apply_projection(w_decay).astype(jnp.float32)
    query_vector = jnp.repeat(unit_rows(query_vector) * DK ** (-0.5), 2, axis=2)
    key = jnp.repeat(unit_rows(key), 2, axis=2)
    beta = jax.nn.sigmoid(beta_raw)
    decay = jnp.exp(-decay_rate * jax.nn.softplus(decay_raw + decay_bias))
    marks = active.T
    readouts = lax.map(one_request, (states, jnp.moveaxis(query_vector, 0, 1), jnp.moveaxis(key, 0, 1), jnp.moveaxis(value, 0, 1), jnp.moveaxis(beta, 0, 1), jnp.moveaxis(decay, 0, 1), active))
    readouts = jnp.moveaxis(readouts, 0, 1)
    mixed = gated_rms_norm(readouts, gate, head_gain).reshape(steps * batch, HEADS * DV)
    summed = jnp.dot(mixed, w_out, preferred_element_type=jnp.float32).reshape(steps, batch, width)
    hidden = rms_scale(embedded.astype(jnp.float32) + summed, final_gain).astype(jnp.bfloat16)
    columns = jnp.arange(VOCAB, dtype=jnp.int32)

    def score_step(item):
        rows, target, mark = item
        logits = jnp.dot(rows, lm_head, preferred_element_type=jnp.float32)
        total = lax.optimization_barrier(jnp.sum(jnp.exp(logits), axis=1))
        picked = lax.optimization_barrier(jnp.sum(jnp.where(columns[None, :] == target[:, None], logits, 0.0), axis=1))
        return jnp.where(mark > 0, picked - jnp.log(total), 0.0)
    scores = lax.map(score_step, (hidden, targets.T, marks))
    return scores.T
```

```python
import functools

import jax
import jax.numpy as jnp
import numpy as np
from jax import lax
from jax.experimental import pallas as pl
from jax.experimental.pallas import tpu as pltpu
from jax.sharding import Mesh
from jax.sharding import PartitionSpec as P

DK = 128
DV = 128
EPS = 1e-06
AXES = ("xl", "c", "y", "z", "xh")
SIZES = (2, 2, 4, 4, 2)
HEAD = ("xl", "c")
BATCH = ("y", "z", "xh")
DEVICES = 128
GROUPS = 32
F32 = jnp.float32
BF16 = jnp.bfloat16


def route(move):
    pairs = []
    for source in range(DEVICES):
        spot = [int(i) for i in np.unravel_index(source, SIZES)]
        pairs.append((source, int(np.ravel_multi_index(move(*spot), SIZES))))
    return pairs


def shift(first, second, hops):
    def move(xl, c, y, z, xh):
        if (first, second)[c] == "y":
            return (xl, c, (y + hops) % 4, z, xh)
        return (xl, c, y, (z + hops) % 4, xh)

    return route(move)


OTHER_CORE = route(lambda xl, c, y, z, xh: (xl, 1 - c, y, z, xh))
OTHER_LOW = route(lambda xl, c, y, z, xh: (1 - xl, c, y, z, xh))
OTHER_HIGH = route(lambda xl, c, y, z, xh: (xl, c, y, z, 1 - xh))
NEAR = [shift("y", "z", k) for k in (1, 3, 2)]
FAR = [shift("z", "y", k) for k in (1, 3, 2)]


def sources():
    held = [[d % GROUPS] for d in range(DEVICES)]
    for stage in ([OTHER_HIGH], NEAR, FAR):
        grown = [list(h) for h in held]
        for pairs in stage:
            for source, target in pairs:
                grown[target].extend(held[source])
        held = grown
    return np.array(held, np.int32)


def front_kernel(
    spot,
    rate,
    offset,
    embedded,
    states,
    w_query,
    w_key,
    w_value,
    w_gate,
    w_beta,
    w_decay,
    w_out,
    input_gain,
    head_gain,
    active,
    give,
    keep,
    normed,
    kq,
    reads,
    beta_all,
    decay_all,
    marks,
    mixed,
    total,
):
    step = pl.program_id(0)
    steps, group, width = embedded.shape
    rows = steps * group

    def contract_last(a, b):
        return lax.dot_general(a, b, (((1,), (1,)), ((), ())), preferred_element_type=F32)

    @pl.when(step == 0)
    def _():
        for t in range(steps):
            e = embedded[t].astype(F32)
            scale = lax.rsqrt(jnp.mean(e * e, axis=-1, keepdims=True) + EPS)
            normed[t * group : (t + 1) * group, :] = (e * scale * input_gain[...]).astype(BF16)
        n = normed[...]
        beta_raw = contract_last(n, w_beta[...]).astype(BF16).astype(F32)
        decay_raw = contract_last(n, w_decay[...]).astype(BF16).astype(F32)
        for h in range(w_beta.shape[0]):
            b = jnp.broadcast_to(beta_raw[:, h : h + 1], (rows, DV))
            d = jnp.broadcast_to(decay_raw[:, h : h + 1], (rows, DV))
            at = spot[1] * w_beta.shape[0] + h
            beta_all[h] = jax.nn.sigmoid(b)
            decay_all[h] = jnp.exp(-rate[at] * jax.nn.softplus(d + offset[at]))
        requests = active.shape[1]
        here = lax.broadcasted_iota(jnp.int32, (group, requests), 1) == (
            spot[0] * group + lax.broadcasted_iota(jnp.int32, (group, requests), 0)
        )
        for t in range(steps):
            line = jnp.broadcast_to(active[t : t + 1, :].astype(F32), (group, requests))
            column = jnp.sum(jnp.where(here, line, 0.0), axis=1, keepdims=True)
            marks[t] = jnp.broadcast_to(column, (group, DV))

    n = normed[...]

    def project(weight):
        return jnp.dot(n, weight[...], preferred_element_type=F32).astype(BF16).astype(F32)

    def unit(x):
        return x * lax.rsqrt(jnp.sum(x * x, axis=-1, keepdims=True) + EPS)

    kq[:rows, :] = unit(project(w_key))
    kq[rows:, :] = unit(project(w_query)) * DK ** (-0.5)
    value = project(w_value)
    gate = project(w_gate)
    k = [kq[t * group : (t + 1) * group, :] for t in range(steps)]
    q = [kq[rows + t * group : rows + (t + 1) * group, :] for t in range(steps)]

    def inner(a, b):
        return jnp.broadcast_to(jnp.sum(a * b, axis=-1, keepdims=True), (group, DV))

    kk = {(t, i): inner(k[t], k[i]) for t in range(steps) for i in range(t)}
    qk = {(t, i): inner(q[t], k[i]) for t in range(steps) for i in range(t + 1)}
    for r in range(group):
        lines = kq[pl.ds(r, 2 * steps, stride=group), :]
        high = lines.astype(BF16).astype(F32)
        both = jnp.concatenate([high, lines - high], axis=0).astype(BF16)
        for h in range(2):
            got = jnp.dot(both, states[r, h], preferred_element_type=F32)
            reads[h, pl.ds(r, 2 * steps, stride=group), :] = got[: 2 * steps] + got[2 * steps :]
    for h in range(2):
        head = 2 * step + h
        coefficient = []
        update = []
        for t in range(steps):
            at = slice(t * group, (t + 1) * group)
            decay = decay_all[head, at, :]
            beta = beta_all[head, at, :]
            mark = marks[t] > 0
            of_key = reads[h, at, :]
            of_query = reads[h, rows + t * group : rows + (t + 1) * group, :]
            if t > 0:
                of_key = start * of_key
                of_query = start * of_query
            for i in range(t):
                of_key = of_key + coefficient[i] * kk[t, i] * update[i]
                of_query = of_query + coefficient[i] * qk[t, i] * update[i]
            u = beta * (value[at, h * DV : (h + 1) * DV] - decay * of_key)
            readout = decay * of_query + qk[t, t] * u
            faded = jnp.where(mark, decay, 1.0)
            start = faded if t == 0 else start * faded
            coefficient = [old * faded for old in coefficient] + [jnp.where(mark, 1.0, 0.0)]
            update.append(u)
            scale = lax.rsqrt(jnp.mean(readout * readout, axis=-1, keepdims=True) + EPS)
            g = gate[at, h * DV : (h + 1) * DV]
            mixed[at, h * DV : (h + 1) * DV] = (
                readout * scale * head_gain[...] * (g * jax.nn.sigmoid(g))
            ).astype(BF16)
    part = jnp.dot(mixed[...], w_out[...], preferred_element_type=F32)

    @pl.when(step == 0)
    def _():
        total[...] = part

    @pl.when(step > 0)
    def _():
        total[...] += part

    @pl.when(step == pl.num_programs(0) - 1)
    def _():
        half = rows // 2
        c = spot[2]
        keep[...] = total[pl.ds(pl.multiple_of(c * half, half), half), :]
        give[...] = total[pl.ds(pl.multiple_of((1 - c) * half, half), half), :].astype(BF16)


def front(spot, rate, offset, embedded, states, wq, wk, wv, wg, wb, wd, wo, ig, hg, active):
    steps, group, width = embedded.shape
    rows, heads = steps * group, states.shape[1]
    key_heads = heads // 2
    whole = lambda *shape: pl.BlockSpec(shape, lambda j, *_: (0,) * len(shape))
    across = lambda cols: pl.BlockSpec((width, cols), lambda j, *_: (0, j))
    return pl.pallas_call(
        front_kernel,
        grid_spec=pltpu.PrefetchScalarGridSpec(
            num_scalar_prefetch=3,
            grid=(key_heads,),
            in_specs=[
                whole(steps, group, width),
                pl.BlockSpec((group, 2, DK, DV), lambda j, *_: (0, j, 0, 0)),
                across(DK),
                across(DK),
                across(2 * DV),
                across(2 * DV),
                whole(heads, width),
                whole(heads, width),
                pl.BlockSpec((2 * DV, width), lambda j, *_: (j, 0)),
                whole(1, width),
                whole(1, DV),
                whole(*active.shape),
            ],
            out_specs=[whole(rows // 2, width), whole(rows // 2, width)],
            scratch_shapes=[
                pltpu.VMEM((rows, width), BF16),
                pltpu.VMEM((2 * rows, DK), F32),
                pltpu.VMEM((2, 2 * rows, DV), F32),
                pltpu.VMEM((heads, rows, DV), F32),
                pltpu.VMEM((heads, rows, DV), F32),
                pltpu.VMEM((steps, group, DV), F32),
                pltpu.VMEM((rows, 2 * DV), BF16),
                pltpu.VMEM((rows, width), F32),
            ],
        ),
        out_shape=[
            jax.ShapeDtypeStruct((rows // 2, width), BF16),
            jax.ShapeDtypeStruct((rows // 2, width), F32),
        ],
        compiler_params=pltpu.CompilerParams(
            dimension_semantics=("arbitrary",), vmem_limit_bytes=32 << 20
        ),
        cost_estimate=pl.CostEstimate(
            flops=2 * rows * width * 4096, bytes_accessed=21 << 20, transcendentals=0
        ),
        name="front",
    )(spot, rate, offset, embedded, states, wq, wk, wv, wg, wb, wd, wo, ig, hg, active)


def score_kernel(bases, hidden, own, other, target, stats, totals, picks):
    step = pl.program_id(0)
    rows, cols = hidden.shape[0], own.shape[1]
    x = hidden[...]
    want = target[...]
    running = jnp.zeros((rows, 128), F32)
    found = jnp.zeros((rows, 128), F32)
    lane = lax.broadcasted_iota(jnp.int32, (rows, 128), 1)
    for which, weight in enumerate((own, other)):
        logits = jnp.dot(x, weight[...], preferred_element_type=F32)
        left = jnp.broadcast_to(want - (bases[which] + step * cols), (rows, 128)) - lane
        for s in range(cols // 128):
            part = logits[:, s * 128 : (s + 1) * 128]
            running = running + jnp.exp(part)
            found = found + jnp.where(left == s * 128, part, 0.0)

    @pl.when(step == 0)
    def _():
        totals[...] = running
        picks[...] = found

    @pl.when(step > 0)
    def _():
        totals[...] += running
        picks[...] += found

    @pl.when(step == pl.num_programs(0) - 1)
    def _():
        sums = jnp.sum(totals[...], axis=1, keepdims=True)
        hits = jnp.sum(picks[...], axis=1, keepdims=True)
        turned = jnp.where(lane == 0, sums, hits).T
        stats[...] = turned[:8, :]


def score(bases, hidden, own, other, target):
    rows, width = hidden.shape
    cols = own.shape[1]
    tile = 256
    return pl.pallas_call(
        score_kernel,
        grid_spec=pltpu.PrefetchScalarGridSpec(
            num_scalar_prefetch=1,
            grid=(cols // tile,),
            in_specs=[
                pl.BlockSpec((rows, width), lambda j, *_: (0, 0)),
                pl.BlockSpec((width, tile), lambda j, *_: (0, j)),
                pl.BlockSpec((width, tile), lambda j, *_: (0, j)),
                pl.BlockSpec((rows, 1), lambda j, *_: (0, 0)),
            ],
            out_specs=pl.BlockSpec((8, rows), lambda j, *_: (0, 0)),
            scratch_shapes=[pltpu.VMEM((rows, 128), F32), pltpu.VMEM((rows, 128), F32)],
        ),
        out_shape=jax.ShapeDtypeStruct((8, rows), F32),
        compiler_params=pltpu.CompilerParams(
            dimension_semantics=("arbitrary",), vmem_limit_bytes=32 << 20
        ),
        cost_estimate=pl.CostEstimate(
            flops=4 * rows * width * cols,
            bytes_accessed=2 * width * (2 * cols + rows),
            transcendentals=2 * rows * cols,
        ),
        name="score",
    )(bases, hidden, own, other, target)


def per_device(
    embedded,
    states,
    w_query,
    w_key,
    w_value,
    w_output_gate,
    w_beta,
    w_decay,
    decay_rate,
    decay_bias,
    head_gain,
    input_gain,
    w_out,
    final_gain,
    lm_head,
    targets,
    active,
):
    steps, group, width = embedded.shape
    cols = lm_head.shape[1]
    me = lax.axis_index(AXES).astype(jnp.int32)
    core = lax.axis_index("c").astype(jnp.int32)
    batch = lax.axis_index(BATCH).astype(jnp.int32)
    head = lax.axis_index(HEAD).astype(jnp.int32)
    send = functools.partial(lax.ppermute, axis_name=AXES)
    far_head = send(lm_head, perm=OTHER_CORE)

    spot = jnp.stack([batch, head, core])
    give, keep = front(
        spot,
        decay_rate,
        decay_bias,
        embedded,
        states,
        w_query,
        w_key,
        w_value,
        w_output_gate,
        w_beta.T,
        w_decay.T,
        w_out,
        input_gain[None],
        head_gain[None],
        active.T,
    )
    pair = (keep + send(give, perm=OTHER_CORE).astype(F32)).astype(BF16)
    summed = pair.astype(F32) + send(pair, perm=OTHER_LOW).astype(F32)
    mine = lax.dynamic_slice_in_dim(embedded, core * (steps // 2), steps // 2, 0)
    y = mine.reshape(-1, width).astype(F32) + summed
    hidden = (
        y * lax.rsqrt(jnp.mean(y * y, axis=-1, keepdims=True) + EPS) * final_gain
    ).astype(BF16)

    block = hidden.shape[0]
    table = sources()
    order = lax.dynamic_index_in_dim(jnp.asarray(table), me, 0, keepdims=False)
    inverse = lax.dynamic_index_in_dim(
        jnp.asarray(np.argsort(table, axis=1).astype(np.int32)), me, 0, keepdims=False
    )
    wanted = lax.dynamic_slice_in_dim(targets.T, core * (steps // 2), steps // 2, 0)
    wanted = jnp.take(wanted.reshape(steps // 2, GROUPS, group), order, axis=1)
    wanted = wanted.transpose(1, 0, 2).reshape(GROUPS * block, 1)

    both = jnp.concatenate([hidden, send(hidden, perm=OTHER_HIGH)], 0)
    near = jnp.concatenate([both] + [send(both, perm=p) for p in NEAR], 0)
    pieces = [near] + [send(near, perm=p) for p in FAR]
    bases = jnp.stack([me * cols, (me ^ GROUPS) * cols])
    size = near.shape[0]
    stats = [
        score(bases, piece, lm_head, far_head, wanted[i * size : (i + 1) * size])[:2]
        for i, piece in enumerate(pieces)
    ]
    stats = jnp.concatenate(stats, 1).reshape(2, GROUPS, block).transpose(1, 0, 2)
    stats = jnp.take(stats.reshape(GROUPS, 2 * block), inverse, axis=0)
    stats = jnp.broadcast_to(stats[None], (4, GROUPS, 2 * block)).reshape(DEVICES, 2 * block)
    stats = lax.all_to_all(stats, AXES, 0, 0, tiled=True)
    stats = jnp.sum(stats.reshape(2, 2, GROUPS, 2, steps // 2, group), axis=(0, 2))
    total, picked = stats[:, 0].reshape(steps, group), stats[:, 1].reshape(steps, group)
    marks = lax.dynamic_slice_in_dim(active.T, batch * group, group, 1)
    return jnp.where(marks > 0, picked - jnp.log(total), 0.0).T


def solution(mesh):
    finer = Mesh(mesh.devices.reshape(SIZES), AXES)
    return jax.shard_map(
        per_device,
        mesh=finer,
        in_specs=(
            P(None, BATCH, None),
            P(BATCH, HEAD, None, None),
            P(None, HEAD),
            P(None, HEAD),
            P(None, HEAD),
            P(None, HEAD),
            P(None, HEAD),
            P(None, HEAD),
            P(),
            P(),
            P(),
            P(),
            P(HEAD, None),
            P(),
            P(None, HEAD + BATCH),
            P(),
            P(),
        ),
        out_specs=P(BATCH, None),
        check_vma=False,
    )
```

```python
import functools

import jax
import jax.numpy as jnp
import numpy as np
from jax import lax
from jax.experimental import pallas as pl
from jax.experimental.pallas import tpu as pltpu
from jax.sharding import Mesh
from jax.sharding import PartitionSpec as P

DK = 128
DV = 128
EPS = 1e-06
AXES = ("xl", "c", "y", "z", "xh")
SIZES = (2, 2, 4, 4, 2)
HEAD = ("xl", "c")
BATCH = ("y", "z", "xh")
DEVICES = 128
GROUPS = 32
F32 = jnp.float32
BF16 = jnp.bfloat16


def route(move):
    pairs = []
    for source in range(DEVICES):
        spot = [int(i) for i in np.unravel_index(source, SIZES)]
        pairs.append((source, int(np.ravel_multi_index(move(*spot), SIZES))))
    return pairs


def shift(first, second, hops):
    def move(xl, c, y, z, xh):
        if (first, second)[c] == "y":
            return (xl, c, (y + hops) % 4, z, xh)
        return (xl, c, y, (z + hops) % 4, xh)

    return route(move)


OTHER_CORE = route(lambda xl, c, y, z, xh: (xl, 1 - c, y, z, xh))
OTHER_LOW = route(lambda xl, c, y, z, xh: (1 - xl, c, y, z, xh))
OTHER_HIGH = route(lambda xl, c, y, z, xh: (xl, c, y, z, 1 - xh))
NEAR = [shift("y", "z", k) for k in (1, 3, 2)]
FAR = [shift("z", "y", k) for k in (1, 3, 2)]


def sources():
    held = [[d % GROUPS] for d in range(DEVICES)]
    for stage in ([OTHER_HIGH], NEAR, FAR):
        grown = [list(h) for h in held]
        for pairs in stage:
            for source, target in pairs:
                grown[target].extend(held[source])
        held = grown
    return np.array(held, np.int32)


def front_kernel(
    spot,
    rate,
    offset,
    embedded,
    states,
    w_query,
    w_key,
    w_value,
    w_gate,
    w_beta,
    w_decay,
    w_out,
    input_gain,
    head_gain,
    active,
    give,
    keep,
    normed,
    kq,
    reads,
    beta_all,
    decay_all,
    marks,
    mixed,
    total,
):
    step = pl.program_id(0)
    steps, group, width = embedded.shape
    rows = steps * group

    def contract_last(a, b):
        return lax.dot_general(a, b, (((1,), (1,)), ((), ())), preferred_element_type=F32)

    @pl.when(step == 0)
    def _():
        for t in range(steps):
            e = embedded[t].astype(F32)
            scale = lax.rsqrt(jnp.mean(e * e, axis=-1, keepdims=True) + EPS)
            normed[t * group : (t + 1) * group, :] = (e * scale * input_gain[...]).astype(BF16)
        n = normed[...]
        beta_raw = contract_last(n, w_beta[...]).astype(BF16).astype(F32)
        decay_raw = contract_last(n, w_decay[...]).astype(BF16).astype(F32)
        for h in range(w_beta.shape[0]):
            b = jnp.broadcast_to(beta_raw[:, h : h + 1], (rows, DV))
            d = jnp.broadcast_to(decay_raw[:, h : h + 1], (rows, DV))
            at = spot[1] * w_beta.shape[0] + h
            beta_all[h] = jax.nn.sigmoid(b)
            decay_all[h] = jnp.exp(-rate[at] * jax.nn.softplus(d + offset[at]))
        requests = active.shape[1]
        here = lax.broadcasted_iota(jnp.int32, (group, requests), 1) == (
            spot[0] * group + lax.broadcasted_iota(jnp.int32, (group, requests), 0)
        )
        for t in range(steps):
            line = jnp.broadcast_to(active[t : t + 1, :].astype(F32), (group, requests))
            column = jnp.sum(jnp.where(here, line, 0.0), axis=1, keepdims=True)
            marks[t] = jnp.broadcast_to(column, (group, DV))

    n = normed[...]

    def project(weight):
        return jnp.dot(n, weight[...], preferred_element_type=F32).astype(BF16).astype(F32)

    def unit(x):
        return x * lax.rsqrt(jnp.sum(x * x, axis=-1, keepdims=True) + EPS)

    kq[:rows, :] = unit(project(w_key))
    kq[rows:, :] = unit(project(w_query)) * DK ** (-0.5)
    value = project(w_value)
    gate = project(w_gate)
    k = [kq[t * group : (t + 1) * group, :] for t in range(steps)]
    q = [kq[rows + t * group : rows + (t + 1) * group, :] for t in range(steps)]

    def inner(a, b):
        return jnp.broadcast_to(jnp.sum(a * b, axis=-1, keepdims=True), (group, DV))

    kk = {(t, i): inner(k[t], k[i]) for t in range(steps) for i in range(t)}
    qk = {(t, i): inner(q[t], k[i]) for t in range(steps) for i in range(t + 1)}
    for r in range(group):
        lines = kq[pl.ds(r, 2 * steps, stride=group), :]
        high = lines.astype(BF16).astype(F32)
        both = jnp.concatenate([high, lines - high], axis=0).astype(BF16)
        for h in range(2):
            got = jnp.dot(both, states[r, h], preferred_element_type=F32)
            reads[h, pl.ds(r, 2 * steps, stride=group), :] = got[: 2 * steps] + got[2 * steps :]
    for h in range(2):
        head = 2 * step + h
        coefficient = []
        update = []
        for t in range(steps):
            at = slice(t * group, (t + 1) * group)
            decay = decay_all[head, at, :]
            beta = beta_all[head, at, :]
            mark = marks[t] > 0
            of_key = reads[h, at, :]
            of_query = reads[h, rows + t * group : rows + (t + 1) * group, :]
            if t > 0:
                of_key = start * of_key
                of_query = start * of_query
            for i in range(t):
                of_key = of_key + coefficient[i] * kk[t, i] * update[i]
                of_query = of_query + coefficient[i] * qk[t, i] * update[i]
            u = beta * (value[at, h * DV : (h + 1) * DV] - decay * of_key)
            readout = decay * of_query + qk[t, t] * u
            faded = jnp.where(mark, decay, 1.0)
            start = faded if t == 0 else start * faded
            coefficient = [old * faded for old in coefficient] + [jnp.where(mark, 1.0, 0.0)]
            update.append(u)
            scale = lax.rsqrt(jnp.mean(readout * readout, axis=-1, keepdims=True) + EPS)
            g = gate[at, h * DV : (h + 1) * DV]
            mixed[at, h * DV : (h + 1) * DV] = (
                readout * scale * head_gain[...] * (g * jax.nn.sigmoid(g))
            ).astype(BF16)
    part = jnp.dot(mixed[...], w_out[...], preferred_element_type=F32)

    @pl.when(step == 0)
    def _():
        total[...] = part

    @pl.when(step > 0)
    def _():
        total[...] += part

    @pl.when(step == pl.num_programs(0) - 1)
    def _():
        half = rows // 2
        c = spot[2]
        keep[...] = total[pl.ds(pl.multiple_of(c * half, half), half), :]
        give[...] = total[pl.ds(pl.multiple_of((1 - c) * half, half), half), :].astype(BF16)


def front(spot, rate, offset, embedded, states, wq, wk, wv, wg, wb, wd, wo, ig, hg, active):
    steps, group, width = embedded.shape
    rows, heads = steps * group, states.shape[1]
    key_heads = heads // 2
    whole = lambda *shape: pl.BlockSpec(shape, lambda j, *_: (0,) * len(shape))
    across = lambda cols: pl.BlockSpec((width, cols), lambda j, *_: (0, j))
    return pl.pallas_call(
        front_kernel,
        grid_spec=pltpu.PrefetchScalarGridSpec(
            num_scalar_prefetch=3,
            grid=(key_heads,),
            in_specs=[
                whole(steps, group, width),
                pl.BlockSpec((group, 2, DK, DV), lambda j, *_: (0, j, 0, 0)),
                across(DK),
                across(DK),
                across(2 * DV),
                across(2 * DV),
                whole(heads, width),
                whole(heads, width),
                pl.BlockSpec((2 * DV, width), lambda j, *_: (j, 0)),
                whole(1, width),
                whole(1, DV),
                whole(*active.shape),
            ],
            out_specs=[whole(rows // 2, width), whole(rows // 2, width)],
            scratch_shapes=[
                pltpu.VMEM((rows, width), BF16),
                pltpu.VMEM((2 * rows, DK), F32),
                pltpu.VMEM((2, 2 * rows, DV), F32),
                pltpu.VMEM((heads, rows, DV), F32),
                pltpu.VMEM((heads, rows, DV), F32),
                pltpu.VMEM((steps, group, DV), F32),
                pltpu.VMEM((rows, 2 * DV), BF16),
                pltpu.VMEM((rows, width), F32),
            ],
        ),
        out_shape=[
            jax.ShapeDtypeStruct((rows // 2, width), BF16),
            jax.ShapeDtypeStruct((rows // 2, width), F32),
        ],
        compiler_params=pltpu.CompilerParams(
            dimension_semantics=("arbitrary",), vmem_limit_bytes=60 << 20
        ),
        cost_estimate=pl.CostEstimate(
            flops=2 * rows * width * 4096, bytes_accessed=21 << 20, transcendentals=0
        ),
        name="front",
    )(spot, rate, offset, embedded, states, wq, wk, wv, wg, wb, wd, wo, ig, hg, active)


TILE = 256


def score_kernel(count, bases, *refs):
    pieces, (own, other, target, stats) = refs[:count], refs[count : count + 4]
    hidden, weights, totals, picks, piece_sems, weight_sems = refs[count + 4 :]
    rows, tiles = hidden.shape[0], weights.shape[0]
    size = rows // count

    def piece_copy(i):
        return pltpu.make_async_copy(
            pieces[i], hidden.at[pl.ds(i * size, size), :], piece_sems.at[i]
        )

    def weight_copy(i, which):
        columns = pl.ds(pl.multiple_of(i * TILE, TILE), TILE)
        return pltpu.make_async_copy(
            (own, other)[which].at[:, columns], weights.at[i, which], weight_sems.at[i, which]
        )

    for i in range(count):
        piece_copy(i).start()
    for i in range(tiles):
        for which in range(2):
            weight_copy(i, which).start()
    totals[...] = jnp.zeros_like(totals)
    picks[...] = jnp.zeros_like(picks)
    for i in range(count):
        piece_copy(i).wait()
    lane = lax.broadcasted_iota(jnp.int32, (rows, 128), 1)

    def body(i, carry):
        x = hidden[...]
        for which in range(2):
            weight_copy(i, which).wait()
            logits = jnp.dot(x, weights[i, which], preferred_element_type=F32)
            left = jnp.broadcast_to(target[...] - (bases[which] + i * TILE), (rows, 128)) - lane
            running = totals[...]
            found = picks[...]
            for s in range(TILE // 128):
                part = logits[:, s * 128 : (s + 1) * 128]
                running = running + jnp.exp(part)
                found = found + jnp.where(left == s * 128, part, 0.0)
            totals[...] = running
            picks[...] = found
        return carry

    lax.fori_loop(0, tiles, body, 0)
    sums = jnp.sum(totals[...], axis=1, keepdims=True)
    hits = jnp.sum(picks[...], axis=1, keepdims=True)
    stats[...] = jnp.where(lane == 0, sums, hits).T[:8, :]


def score(bases, pieces, own, other, target):
    size, width = pieces[0].shape
    count, cols = len(pieces), own.shape[1]
    rows = size * count
    raw = pl.BlockSpec(memory_space=pltpu.HBM)
    return pl.pallas_call(
        functools.partial(score_kernel, count),
        grid_spec=pltpu.PrefetchScalarGridSpec(
            num_scalar_prefetch=1,
            grid=(1,),
            in_specs=[raw] * (count + 2) + [pl.BlockSpec((rows, 1), lambda j, *_: (0, 0))],
            out_specs=pl.BlockSpec((8, rows), lambda j, *_: (0, 0)),
            scratch_shapes=[
                pltpu.VMEM((rows, width), BF16),
                pltpu.VMEM((cols // TILE, 2, width, TILE), BF16),
                pltpu.VMEM((rows, 128), F32),
                pltpu.VMEM((rows, 128), F32),
                pltpu.SemaphoreType.DMA((count,)),
                pltpu.SemaphoreType.DMA((cols // TILE, 2)),
            ],
        ),
        out_shape=jax.ShapeDtypeStruct((8, rows), F32),
        compiler_params=pltpu.CompilerParams(
            dimension_semantics=("arbitrary",), vmem_limit_bytes=60 << 20
        ),
        cost_estimate=pl.CostEstimate(
            flops=4 * rows * width * cols,
            bytes_accessed=2 * width * (2 * cols + rows),
            transcendentals=2 * rows * cols,
        ),
        name="score",
    )(bases, *pieces, own, other, target)


def per_device(
    embedded,
    states,
    w_query,
    w_key,
    w_value,
    w_output_gate,
    w_beta,
    w_decay,
    decay_rate,
    decay_bias,
    head_gain,
    input_gain,
    w_out,
    final_gain,
    lm_head,
    targets,
    active,
):
    steps, group, width = embedded.shape
    cols = lm_head.shape[1]
    me = lax.axis_index(AXES).astype(jnp.int32)
    core = lax.axis_index("c").astype(jnp.int32)
    batch = lax.axis_index(BATCH).astype(jnp.int32)
    head = lax.axis_index(HEAD).astype(jnp.int32)
    send = functools.partial(lax.ppermute, axis_name=AXES)
    far_head = send(lm_head, perm=OTHER_CORE)

    spot = jnp.stack([batch, head, core])
    give, keep = front(
        spot,
        decay_rate,
        decay_bias,
        embedded,
        states,
        w_query,
        w_key,
        w_value,
        w_output_gate,
        w_beta.T,
        w_decay.T,
        w_out,
        input_gain[None],
        head_gain[None],
        active.T,
    )
    block = keep.shape[0]
    table = sources()
    order = lax.dynamic_index_in_dim(jnp.asarray(table), me, 0, keepdims=False)
    inverse = lax.dynamic_index_in_dim(
        jnp.asarray(np.argsort(table, axis=1).astype(np.int32)), me, 0, keepdims=False
    )
    pair = (keep + send(give, perm=OTHER_CORE).astype(F32)).astype(BF16)
    bases = jnp.stack([me * cols, (me ^ GROUPS) * cols])
    pair, order, inverse, bases = lax.optimization_barrier((pair, order, inverse, bases))
    wanted = lax.dynamic_slice_in_dim(targets.T, core * (steps // 2), steps // 2, 0)
    wanted = jnp.take(wanted.reshape(steps // 2, GROUPS, group), order, axis=1)
    wanted = wanted.transpose(1, 0, 2).reshape(GROUPS * block, 1)
    from_low = send(pair, perm=OTHER_LOW)
    from_low, wanted, inverse = lax.optimization_barrier((from_low, wanted, inverse))
    summed = pair.astype(F32) + from_low.astype(F32)
    mine = lax.dynamic_slice_in_dim(embedded, core * (steps // 2), steps // 2, 0)
    y = mine.reshape(-1, width).astype(F32) + summed
    hidden = (
        y * lax.rsqrt(jnp.mean(y * y, axis=-1, keepdims=True) + EPS) * final_gain
    ).astype(BF16)

    both = jnp.concatenate([hidden, send(hidden, perm=OTHER_HIGH)], 0)
    near = jnp.concatenate([both] + [send(both, perm=p) for p in NEAR], 0)
    size = near.shape[0]
    forth, back = send(near, perm=FAR[0]), send(near, perm=FAR[1])
    stats = [score(bases, [near], lm_head, far_head, wanted[:size])]
    near, first = lax.optimization_barrier((near, stats[0]))
    facing = send(near, perm=FAR[2])
    stats = [first]
    stats.append(score(bases, [forth, back], lm_head, far_head, wanted[size : 3 * size]))
    stats.append(score(bases, [facing], lm_head, far_head, wanted[3 * size :]))
    stats = [part[:2] for part in stats]
    stats = jnp.concatenate(stats, 1).reshape(2, GROUPS, block).transpose(1, 0, 2)
    stats = jnp.take(stats.reshape(GROUPS, 2 * block), inverse, axis=0)
    stats = jnp.broadcast_to(stats[None], (4, GROUPS, 2 * block)).reshape(DEVICES, 2 * block)
    stats = lax.all_to_all(stats, AXES, 0, 0, tiled=True)
    stats = jnp.sum(stats.reshape(2, 2, GROUPS, 2, steps // 2, group), axis=(0, 2))
    total, picked = stats[:, 0].reshape(steps, group), stats[:, 1].reshape(steps, group)
    marks = lax.dynamic_slice_in_dim(active.T, batch * group, group, 1)
    return jnp.where(marks > 0, picked - jnp.log(total), 0.0).T


def solution(mesh):
    finer = Mesh(mesh.devices.reshape(SIZES), AXES)
    return jax.shard_map(
        per_device,
        mesh=finer,
        in_specs=(
            P(None, BATCH, None),
            P(BATCH, HEAD, None, None),
            P(None, HEAD),
            P(None, HEAD),
            P(None, HEAD),
            P(None, HEAD),
            P(None, HEAD),
            P(None, HEAD),
            P(),
            P(),
            P(),
            P(),
            P(HEAD, None),
            P(),
            P(None, HEAD + BATCH),
            P(),
            P(),
        ),
        out_specs=P(BATCH, None),
        check_vma=False,
    )
```

```python
import functools

import jax
import jax.numpy as jnp
import numpy as np
from jax import lax
from jax.experimental import pallas as pl
from jax.experimental.pallas import tpu as pltpu
from jax.sharding import Mesh
from jax.sharding import PartitionSpec as P

DK = 128
DV = 128
EPS = 1e-06
AXES = ("xl", "c", "y", "z", "xh")
SIZES = (2, 2, 4, 4, 2)
HEAD = ("xl", "c")
BATCH = ("y", "z", "xh")
DEVICES = 128
GROUPS = 32
F32 = jnp.float32
BF16 = jnp.bfloat16


def route(move):
    pairs = []
    for source in range(DEVICES):
        spot = [int(i) for i in np.unravel_index(source, SIZES)]
        pairs.append((source, int(np.ravel_multi_index(move(*spot), SIZES))))
    return pairs


def shift(first, second, hops):
    def move(xl, c, y, z, xh):
        if (first, second)[c] == "y":
            return (xl, c, (y + hops) % 4, z, xh)
        return (xl, c, y, (z + hops) % 4, xh)

    return route(move)


OTHER_CORE = route(lambda xl, c, y, z, xh: (xl, 1 - c, y, z, xh))
OTHER_LOW = route(lambda xl, c, y, z, xh: (1 - xl, c, y, z, xh))
OTHER_HIGH = route(lambda xl, c, y, z, xh: (xl, c, y, z, 1 - xh))
NEAR = [shift("y", "z", k) for k in (1, 3, 2)]
FAR = [shift("z", "y", k) for k in (1, 3, 2)]


def sources():
    held = [[d % GROUPS] for d in range(DEVICES)]
    for stage in ([OTHER_HIGH], NEAR, FAR):
        grown = [list(h) for h in held]
        for pairs in stage:
            for source, target in pairs:
                grown[target].extend(held[source])
        held = grown
    return np.array(held, np.int32)


def front_kernel(
    spot,
    rate,
    offset,
    embedded,
    states,
    w_query,
    w_key,
    w_value,
    w_gate,
    w_beta,
    w_decay,
    w_out,
    input_gain,
    head_gain,
    active,
    give,
    keep,
    normed,
    kq,
    reads,
    beta_all,
    decay_all,
    marks,
    mixed,
    total,
):
    step = pl.program_id(0)
    steps, group, width = embedded.shape
    rows = steps * group

    def contract_last(a, b):
        return lax.dot_general(a, b, (((1,), (1,)), ((), ())), preferred_element_type=F32)

    @pl.when(step == 0)
    def _():
        for t in range(steps):
            e = embedded[t].astype(F32)
            scale = lax.rsqrt(jnp.mean(e * e, axis=-1, keepdims=True) + EPS)
            normed[t * group : (t + 1) * group, :] = (e * scale * input_gain[...]).astype(BF16)
        n = normed[...]
        beta_raw = contract_last(n, w_beta[...]).astype(BF16).astype(F32)
        decay_raw = contract_last(n, w_decay[...]).astype(BF16).astype(F32)
        for h in range(w_beta.shape[0]):
            b = jnp.broadcast_to(beta_raw[:, h : h + 1], (rows, DV))
            d = jnp.broadcast_to(decay_raw[:, h : h + 1], (rows, DV))
            at = spot[1] * w_beta.shape[0] + h
            beta_all[h] = jax.nn.sigmoid(b)
            decay_all[h] = jnp.exp(-rate[at] * jax.nn.softplus(d + offset[at]))
        requests = active.shape[1]
        here = lax.broadcasted_iota(jnp.int32, (group, requests), 1) == (
            spot[0] * group + lax.broadcasted_iota(jnp.int32, (group, requests), 0)
        )
        for t in range(steps):
            line = jnp.broadcast_to(active[t : t + 1, :].astype(F32), (group, requests))
            column = jnp.sum(jnp.where(here, line, 0.0), axis=1, keepdims=True)
            marks[t] = jnp.broadcast_to(column, (group, DV))

    n = normed[...]

    def project(weight):
        return jnp.dot(n, weight[...], preferred_element_type=F32).astype(BF16).astype(F32)

    def unit(x):
        return x * lax.rsqrt(jnp.sum(x * x, axis=-1, keepdims=True) + EPS)

    kq[:rows, :] = unit(project(w_key))
    kq[rows:, :] = unit(project(w_query)) * DK ** (-0.5)
    value = project(w_value)
    gate = project(w_gate)
    k = [kq[t * group : (t + 1) * group, :] for t in range(steps)]
    q = [kq[rows + t * group : rows + (t + 1) * group, :] for t in range(steps)]

    def inner(a, b):
        return jnp.broadcast_to(jnp.sum(a * b, axis=-1, keepdims=True), (group, DV))

    kk = {(t, i): inner(k[t], k[i]) for t in range(steps) for i in range(t)}
    qk = {(t, i): inner(q[t], k[i]) for t in range(steps) for i in range(t + 1)}
    for r in range(group):
        lines = kq[pl.ds(r, 2 * steps, stride=group), :]
        high = lines.astype(BF16).astype(F32)
        both = jnp.concatenate([high, lines - high], axis=0).astype(BF16)
        for h in range(2):
            got = jnp.dot(both, states[r, h], preferred_element_type=F32)
            reads[h, pl.ds(r, 2 * steps, stride=group), :] = got[: 2 * steps] + got[2 * steps :]
    for h in range(2):
        head = 2 * step + h
        coefficient = []
        update = []
        for t in range(steps):
            at = slice(t * group, (t + 1) * group)
            decay = decay_all[head, at, :]
            beta = beta_all[head, at, :]
            mark = marks[t] > 0
            of_key = reads[h, at, :]
            of_query = reads[h, rows + t * group : rows + (t + 1) * group, :]
            if t > 0:
                of_key = start * of_key
                of_query = start * of_query
            for i in range(t):
                of_key = of_key + coefficient[i] * kk[t, i] * update[i]
                of_query = of_query + coefficient[i] * qk[t, i] * update[i]
            u = beta * (value[at, h * DV : (h + 1) * DV] - decay * of_key)
            readout = decay * of_query + qk[t, t] * u
            faded = jnp.where(mark, decay, 1.0)
            start = faded if t == 0 else start * faded
            coefficient = [old * faded for old in coefficient] + [jnp.where(mark, 1.0, 0.0)]
            update.append(u)
            scale = lax.rsqrt(jnp.mean(readout * readout, axis=-1, keepdims=True) + EPS)
            g = gate[at, h * DV : (h + 1) * DV]
            mixed[at, h * DV : (h + 1) * DV] = (
                readout * scale * head_gain[...] * (g * jax.nn.sigmoid(g))
            ).astype(BF16)
    part = jnp.dot(mixed[...], w_out[...], preferred_element_type=F32)

    @pl.when(step == 0)
    def _():
        total[...] = part

    @pl.when(step > 0)
    def _():
        total[...] += part

    @pl.when(step == pl.num_programs(0) - 1)
    def _():
        half = rows // 2
        c = spot[2]
        keep[...] = total[pl.ds(pl.multiple_of(c * half, half), half), :]
        give[...] = total[pl.ds(pl.multiple_of((1 - c) * half, half), half), :].astype(BF16)


def front(spot, rate, offset, embedded, states, wq, wk, wv, wg, wb, wd, wo, ig, hg, active):
    steps, group, width = embedded.shape
    rows, heads = steps * group, states.shape[1]
    key_heads = heads // 2
    whole = lambda *shape: pl.BlockSpec(shape, lambda j, *_: (0,) * len(shape))
    across = lambda cols: pl.BlockSpec((width, cols), lambda j, *_: (0, j))
    return pl.pallas_call(
        front_kernel,
        grid_spec=pltpu.PrefetchScalarGridSpec(
            num_scalar_prefetch=3,
            grid=(key_heads,),
            in_specs=[
                whole(steps, group, width),
                pl.BlockSpec((group, 2, DK, DV), lambda j, *_: (0, j, 0, 0)),
                across(DK),
                across(DK),
                across(2 * DV),
                across(2 * DV),
                whole(heads, width),
                whole(heads, width),
                pl.BlockSpec((2 * DV, width), lambda j, *_: (j, 0)),
                whole(1, width),
                whole(1, DV),
                whole(*active.shape),
            ],
            out_specs=[whole(rows // 2, width), whole(rows // 2, width)],
            scratch_shapes=[
                pltpu.VMEM((rows, width), BF16),
                pltpu.VMEM((2 * rows, DK), F32),
                pltpu.VMEM((2, 2 * rows, DV), F32),
                pltpu.VMEM((heads, rows, DV), F32),
                pltpu.VMEM((heads, rows, DV), F32),
                pltpu.VMEM((steps, group, DV), F32),
                pltpu.VMEM((rows, 2 * DV), BF16),
                pltpu.VMEM((rows, width), F32),
            ],
        ),
        out_shape=[
            jax.ShapeDtypeStruct((rows // 2, width), BF16),
            jax.ShapeDtypeStruct((rows // 2, width), F32),
        ],
        compiler_params=pltpu.CompilerParams(
            dimension_semantics=("arbitrary",), vmem_limit_bytes=60 << 20
        ),
        cost_estimate=pl.CostEstimate(
            flops=2 * rows * width * 4096, bytes_accessed=21 << 20, transcendentals=0
        ),
        name="front",
    )(spot, rate, offset, embedded, states, wq, wk, wv, wg, wb, wd, wo, ig, hg, active)


TILE = 512


def score_kernel(count, bases, *refs):
    pieces, (vocabulary, target, stats) = refs[:count], refs[count:]
    size, cols = pieces[0].shape[0], vocabulary.shape[2]
    for p in range(count):
        at = slice(p * size, (p + 1) * size)
        lane = lax.broadcasted_iota(jnp.int32, (size, 128), 1)
        running = jnp.zeros((size, 128), F32)
        found = jnp.zeros((size, 128), F32)
        for start in range(0, cols, TILE):
            for which in range(2):
                logits = jnp.dot(
                    pieces[p][...],
                    vocabulary[which, :, start : start + TILE],
                    preferred_element_type=F32,
                )
                left = jnp.broadcast_to(target[at, :] - (bases[which] + start), (size, 128)) - lane
                for s in range(0, TILE, 128):
                    part = logits[:, s : s + 128]
                    running = running + jnp.exp(part)
                    found = found + jnp.where(left == s, part, 0.0)
        sums = jnp.sum(running, axis=1, keepdims=True)
        hits = jnp.sum(found, axis=1, keepdims=True)
        stats[:, at] = jnp.where(lane == 0, sums, hits).T[:8, :]


def gather_kernel(own, other, both, sems):
    copies = [
        pltpu.make_async_copy(source, both.at[i], sems.at[i])
        for i, source in enumerate((own, other))
    ]
    for copy in copies:
        copy.start()
    for copy in copies:
        copy.wait()


def bring_in(own, other):
    return pl.pallas_call(
        gather_kernel,
        in_specs=[pl.BlockSpec(memory_space=pltpu.HBM)] * 2,
        out_specs=pl.BlockSpec(memory_space=pltpu.VMEM),
        scratch_shapes=[pltpu.SemaphoreType.DMA((2,))],
        out_shape=jax.ShapeDtypeStruct((2, *own.shape), own.dtype),
        compiler_params=pltpu.CompilerParams(vmem_limit_bytes=12 << 20),
        cost_estimate=pl.CostEstimate(
            flops=0, bytes_accessed=4 * own.size, transcendentals=0
        ),
        name="bring_in",
    )(own, other)


def score(bases, pieces, vocabulary, target):
    size, width = pieces[0].shape
    count, cols = len(pieces), vocabulary.shape[2]
    rows = size * count
    near = pl.BlockSpec(memory_space=pltpu.VMEM)
    return pl.pallas_call(
        functools.partial(score_kernel, count),
        grid_spec=pltpu.PrefetchScalarGridSpec(
            num_scalar_prefetch=1,
            grid=(),
            in_specs=[near] * (count + 2),
            out_specs=near,
        ),
        out_shape=jax.ShapeDtypeStruct((8, rows), F32),
        compiler_params=pltpu.CompilerParams(vmem_limit_bytes=20 << 20),
        cost_estimate=pl.CostEstimate(
            flops=4 * rows * width * cols,
            bytes_accessed=2 * width * (2 * cols + rows),
            transcendentals=2 * rows * cols,
        ),
        name="score",
    )(bases, *pieces, vocabulary, target)


def per_device(
    embedded,
    states,
    w_query,
    w_key,
    w_value,
    w_output_gate,
    w_beta,
    w_decay,
    decay_rate,
    decay_bias,
    head_gain,
    input_gain,
    w_out,
    final_gain,
    lm_head,
    targets,
    active,
):
    steps, group, width = embedded.shape
    cols = lm_head.shape[1]
    me = lax.axis_index(AXES).astype(jnp.int32)
    core = lax.axis_index("c").astype(jnp.int32)
    batch = lax.axis_index(BATCH).astype(jnp.int32)
    head = lax.axis_index(HEAD).astype(jnp.int32)
    send = functools.partial(lax.ppermute, axis_name=AXES)
    far_head = send(lm_head, perm=OTHER_CORE)

    spot = jnp.stack([batch, head, core])
    give, keep = front(
        spot,
        decay_rate,
        decay_bias,
        embedded,
        states,
        w_query,
        w_key,
        w_value,
        w_output_gate,
        w_beta.T,
        w_decay.T,
        w_out,
        input_gain[None],
        head_gain[None],
        active.T,
    )
    block = keep.shape[0]
    table = sources()
    order = lax.dynamic_index_in_dim(jnp.asarray(table), me, 0, keepdims=False)
    inverse = lax.dynamic_index_in_dim(
        jnp.asarray(np.argsort(table, axis=1).astype(np.int32)), me, 0, keepdims=False
    )
    pair = (keep + send(give, perm=OTHER_CORE).astype(F32)).astype(BF16)
    bases = jnp.stack([me * cols, (me ^ GROUPS) * cols])
    pair, order, inverse, bases = lax.optimization_barrier((pair, order, inverse, bases))
    wanted = lax.dynamic_slice_in_dim(targets.T, core * (steps // 2), steps // 2, 0)
    wanted = jnp.take(wanted.reshape(steps // 2, GROUPS, group), order, axis=1)
    wanted = wanted.transpose(1, 0, 2).reshape(GROUPS * block, 1)
    from_low = send(pair, perm=OTHER_LOW)
    from_low, wanted, inverse = lax.optimization_barrier((from_low, wanted, inverse))
    summed = pair.astype(F32) + from_low.astype(F32)
    mine = lax.dynamic_slice_in_dim(embedded, core * (steps // 2), steps // 2, 0)
    y = mine.reshape(-1, width).astype(F32) + summed
    hidden = (
        y * lax.rsqrt(jnp.mean(y * y, axis=-1, keepdims=True) + EPS) * final_gain
    ).astype(BF16)

    both = jnp.concatenate([hidden, send(hidden, perm=OTHER_HIGH)], 0)
    near = jnp.concatenate([both] + [send(both, perm=p) for p in NEAR], 0)
    size = near.shape[0]
    forth, back = send(near, perm=FAR[0]), send(near, perm=FAR[1])
    far_head, near = lax.optimization_barrier((far_head, near))
    vocabulary = bring_in(lm_head, far_head)
    near, vocabulary = lax.optimization_barrier((near, vocabulary))
    facing = send(near, perm=FAR[2])
    stats = [score(bases, [near], vocabulary, wanted[:size])]
    later, first = lax.optimization_barrier((wanted[size : 3 * size], stats[0]))
    stats = [first, score(bases, [forth, back], vocabulary, later)]
    stats.append(score(bases, [facing], vocabulary, wanted[3 * size :]))
    stats = [part[:2] for part in stats]
    stats = jnp.concatenate(stats, 1).reshape(2, GROUPS, block).transpose(1, 0, 2)
    stats = jnp.take(stats.reshape(GROUPS, 2 * block), inverse, axis=0)
    stats = jnp.broadcast_to(stats[None], (4, GROUPS, 2 * block)).reshape(DEVICES, 2 * block)
    stats = lax.all_to_all(stats, AXES, 0, 0, tiled=True)
    stats = jnp.sum(stats.reshape(2, 2, GROUPS, 2, steps // 2, group), axis=(0, 2))
    total, picked = stats[:, 0].reshape(steps, group), stats[:, 1].reshape(steps, group)
    marks = lax.dynamic_slice_in_dim(active.T, batch * group, group, 1)
    return jnp.where(marks > 0, picked - jnp.log(total), 0.0).T


def solution(mesh):
    finer = Mesh(mesh.devices.reshape(SIZES), AXES)
    return jax.shard_map(
        per_device,
        mesh=finer,
        in_specs=(
            P(None, BATCH, None),
            P(BATCH, HEAD, None, None),
            P(None, HEAD),
            P(None, HEAD),
            P(None, HEAD),
            P(None, HEAD),
            P(None, HEAD),
            P(None, HEAD),
            P(),
            P(),
            P(),
            P(),
            P(HEAD, None),
            P(),
            P(None, HEAD + BATCH),
            P(),
            P(),
        ),
        out_specs=P(BATCH, None),
        check_vma=False,
    )
```

```python
import functools

import jax
import jax.numpy as jnp
import numpy as np
from jax import lax
from jax.experimental import pallas as pl
from jax.experimental.pallas import tpu as pltpu
from jax.sharding import Mesh
from jax.sharding import PartitionSpec as P

DK = 128
DV = 128
EPS = 1e-06
AXES = ("xl", "c", "y", "z", "xh")
SIZES = (2, 2, 4, 4, 2)
HEAD = ("xl", "c")
BATCH = ("y", "z", "xh")
DEVICES = 128
GROUPS = 32
F32 = jnp.float32
BF16 = jnp.bfloat16


def route(move):
    pairs = []
    for source in range(DEVICES):
        spot = [int(i) for i in np.unravel_index(source, SIZES)]
        pairs.append((source, int(np.ravel_multi_index(move(*spot), SIZES))))
    return pairs


def shift(first, second, hops):
    def move(xl, c, y, z, xh):
        if (first, second)[c] == "y":
            return (xl, c, (y + hops) % 4, z, xh)
        return (xl, c, y, (z + hops) % 4, xh)

    return route(move)


OTHER_CORE = route(lambda xl, c, y, z, xh: (xl, 1 - c, y, z, xh))
OTHER_LOW = route(lambda xl, c, y, z, xh: (1 - xl, c, y, z, xh))
OTHER_HIGH = route(lambda xl, c, y, z, xh: (xl, c, y, z, 1 - xh))
NEAR = [shift("y", "z", k) for k in (1, 3, 2)]
FAR = [shift("z", "y", k) for k in (1, 3, 2)]


def sources():
    held = [[d % GROUPS] for d in range(DEVICES)]
    for stage in ([OTHER_HIGH], NEAR, FAR):
        grown = [list(h) for h in held]
        for pairs in stage:
            for source, target in pairs:
                grown[target].extend(held[source])
        held = grown
    return np.array(held, np.int32)


def front_kernel(
    spot,
    rate,
    offset,
    embedded,
    states,
    w_query,
    w_key,
    w_value,
    w_gate,
    w_beta,
    w_decay,
    w_out,
    input_gain,
    head_gain,
    active,
    give,
    keep,
    normed,
    kq,
    reads,
    beta_all,
    decay_all,
    marks,
    mixed,
    total,
):
    step = pl.program_id(0)
    steps, group, width = embedded.shape
    rows = steps * group

    def contract_last(a, b):
        return lax.dot_general(a, b, (((1,), (1,)), ((), ())), preferred_element_type=F32)

    @pl.when(step == 0)
    def _():
        for t in range(steps):
            e = embedded[t].astype(F32)
            scale = lax.rsqrt(jnp.mean(e * e, axis=-1, keepdims=True) + EPS)
            normed[t * group : (t + 1) * group, :] = (e * scale * input_gain[...]).astype(BF16)
        n = normed[...]
        beta_raw = contract_last(n, w_beta[...]).astype(BF16).astype(F32)
        decay_raw = contract_last(n, w_decay[...]).astype(BF16).astype(F32)
        for h in range(w_beta.shape[0]):
            b = jnp.broadcast_to(beta_raw[:, h : h + 1], (rows, DV))
            d = jnp.broadcast_to(decay_raw[:, h : h + 1], (rows, DV))
            at = spot[1] * w_beta.shape[0] + h
            beta_all[h] = jax.nn.sigmoid(b)
            decay_all[h] = jnp.exp(-rate[at] * jax.nn.softplus(d + offset[at]))
        requests = active.shape[1]
        here = lax.broadcasted_iota(jnp.int32, (group, requests), 1) == (
            spot[0] * group + lax.broadcasted_iota(jnp.int32, (group, requests), 0)
        )
        for t in range(steps):
            line = jnp.broadcast_to(active[t : t + 1, :].astype(F32), (group, requests))
            column = jnp.sum(jnp.where(here, line, 0.0), axis=1, keepdims=True)
            marks[t] = jnp.broadcast_to(column, (group, DV))

    n = normed[...]

    def project(weight):
        return jnp.dot(n, weight[...], preferred_element_type=F32).astype(BF16).astype(F32)

    def unit(x):
        return x * lax.rsqrt(jnp.sum(x * x, axis=-1, keepdims=True) + EPS)

    kq[:rows, :] = unit(project(w_key))
    kq[rows:, :] = unit(project(w_query)) * DK ** (-0.5)
    value = project(w_value)
    gate = project(w_gate)
    k = [kq[t * group : (t + 1) * group, :] for t in range(steps)]
    q = [kq[rows + t * group : rows + (t + 1) * group, :] for t in range(steps)]

    def inner(a, b):
        return jnp.broadcast_to(jnp.sum(a * b, axis=-1, keepdims=True), (group, DV))

    kk = {(t, i): inner(k[t], k[i]) for t in range(steps) for i in range(t)}
    qk = {(t, i): inner(q[t], k[i]) for t in range(steps) for i in range(t + 1)}
    for r in range(group):
        lines = kq[pl.ds(r, 2 * steps, stride=group), :]
        high = lines.astype(BF16).astype(F32)
        both = jnp.concatenate([high, lines - high], axis=0).astype(BF16)
        for h in range(2):
            got = jnp.dot(both, states[r, h], preferred_element_type=F32)
            reads[h, pl.ds(r, 2 * steps, stride=group), :] = got[: 2 * steps] + got[2 * steps :]
    for h in range(2):
        head = 2 * step + h
        coefficient = []
        update = []
        for t in range(steps):
            at = slice(t * group, (t + 1) * group)
            decay = decay_all[head, at, :]
            beta = beta_all[head, at, :]
            mark = marks[t] > 0
            of_key = reads[h, at, :]
            of_query = reads[h, rows + t * group : rows + (t + 1) * group, :]
            if t > 0:
                of_key = start * of_key
                of_query = start * of_query
            for i in range(t):
                of_key = of_key + coefficient[i] * kk[t, i] * update[i]
                of_query = of_query + coefficient[i] * qk[t, i] * update[i]
            u = beta * (value[at, h * DV : (h + 1) * DV] - decay * of_key)
            readout = decay * of_query + qk[t, t] * u
            faded = jnp.where(mark, decay, 1.0)
            start = faded if t == 0 else start * faded
            coefficient = [old * faded for old in coefficient] + [jnp.where(mark, 1.0, 0.0)]
            update.append(u)
            scale = lax.rsqrt(jnp.mean(readout * readout, axis=-1, keepdims=True) + EPS)
            g = gate[at, h * DV : (h + 1) * DV]
            mixed[at, h * DV : (h + 1) * DV] = (
                readout * scale * head_gain[...] * (g * jax.nn.sigmoid(g))
            ).astype(BF16)
    part = jnp.dot(mixed[...], w_out[...], preferred_element_type=F32)

    @pl.when(step == 0)
    def _():
        total[...] = part

    @pl.when(step > 0)
    def _():
        total[...] += part

    @pl.when(step == pl.num_programs(0) - 1)
    def _():
        half = rows // 2
        c = spot[2]
        keep[...] = total[pl.ds(pl.multiple_of(c * half, half), half), :]
        give[...] = total[pl.ds(pl.multiple_of((1 - c) * half, half), half), :].astype(BF16)


def front(spot, rate, offset, embedded, states, wq, wk, wv, wg, wb, wd, wo, ig, hg, active):
    steps, group, width = embedded.shape
    rows, heads = steps * group, states.shape[1]
    key_heads = heads // 2
    whole = lambda *shape: pl.BlockSpec(shape, lambda j, *_: (0,) * len(shape))
    across = lambda cols: pl.BlockSpec((width, cols), lambda j, *_: (0, j))
    return pl.pallas_call(
        front_kernel,
        grid_spec=pltpu.PrefetchScalarGridSpec(
            num_scalar_prefetch=3,
            grid=(key_heads,),
            in_specs=[
                whole(steps, group, width),
                pl.BlockSpec((group, 2, DK, DV), lambda j, *_: (0, j, 0, 0)),
                across(DK),
                across(DK),
                across(2 * DV),
                across(2 * DV),
                whole(heads, width),
                whole(heads, width),
                pl.BlockSpec((2 * DV, width), lambda j, *_: (j, 0)),
                whole(1, width),
                whole(1, DV),
                whole(*active.shape),
            ],
            out_specs=[whole(rows // 2, width), whole(rows // 2, width)],
            scratch_shapes=[
                pltpu.VMEM((rows, width), BF16),
                pltpu.VMEM((2 * rows, DK), F32),
                pltpu.VMEM((2, 2 * rows, DV), F32),
                pltpu.VMEM((heads, rows, DV), F32),
                pltpu.VMEM((heads, rows, DV), F32),
                pltpu.VMEM((steps, group, DV), F32),
                pltpu.VMEM((rows, 2 * DV), BF16),
                pltpu.VMEM((rows, width), F32),
            ],
        ),
        out_shape=[
            jax.ShapeDtypeStruct((rows // 2, width), BF16),
            jax.ShapeDtypeStruct((rows // 2, width), F32),
        ],
        compiler_params=pltpu.CompilerParams(
            dimension_semantics=("arbitrary",), vmem_limit_bytes=60 << 20
        ),
        cost_estimate=pl.CostEstimate(
            flops=2 * rows * width * 4096, bytes_accessed=21 << 20, transcendentals=0
        ),
        name="front",
    )(spot, rate, offset, embedded, states, wq, wk, wv, wg, wb, wd, wo, ig, hg, active)


TILE = 512
BLOCK = 256


def score_kernel(count, offset, bases, *refs):
    parts, (vocabulary, target, stats) = refs[:count], refs[count:]
    cols = vocabulary.shape[2]
    if parts[0].shape[0] < BLOCK:
        pieces = [jnp.concatenate([part[...] for part in parts], axis=0)]
    else:
        pieces = [part[...] for part in parts]
    size = pieces[0].shape[0]
    for p, piece in enumerate(pieces):
        at = slice(p * size, (p + 1) * size)
        want = target[offset + p * size : offset + (p + 1) * size, :]
        lane = lax.broadcasted_iota(jnp.int32, (size, 128), 1)
        running = jnp.zeros((size, 128), F32)
        found = jnp.zeros((size, 128), F32)
        for start in range(0, cols, TILE):
            for which in range(2):
                logits = jnp.dot(
                    piece, vocabulary[which, :, start : start + TILE], preferred_element_type=F32
                )
                left = jnp.broadcast_to(want - (bases[which] + start), (size, 128)) - lane
                for s in range(0, TILE, 128):
                    part = logits[:, s : s + 128]
                    running = running + jnp.exp(part)
                    found = found + jnp.where(left == s, part, 0.0)
        sums = jnp.sum(running, axis=1, keepdims=True)
        hits = jnp.sum(found, axis=1, keepdims=True)
        stats[:, at] = jnp.where(lane == 0, sums, hits).T[:8, :]


def gather_kernel(own, other, both, sems):
    copies = [
        pltpu.make_async_copy(source, both.at[i], sems.at[i])
        for i, source in enumerate((own, other))
    ]
    for copy in copies:
        copy.start()
    for copy in copies:
        copy.wait()


def bring_in(own, other):
    return pl.pallas_call(
        gather_kernel,
        in_specs=[pl.BlockSpec(memory_space=pltpu.HBM)] * 2,
        out_specs=pl.BlockSpec(memory_space=pltpu.VMEM),
        scratch_shapes=[pltpu.SemaphoreType.DMA((2,))],
        out_shape=jax.ShapeDtypeStruct((2, *own.shape), own.dtype),
        compiler_params=pltpu.CompilerParams(vmem_limit_bytes=12 << 20),
        cost_estimate=pl.CostEstimate(
            flops=0, bytes_accessed=4 * own.size, transcendentals=0
        ),
        name="bring_in",
    )(own, other)


def score(bases, pieces, vocabulary, target, offset):
    size, width = pieces[0].shape
    count, cols = len(pieces), vocabulary.shape[2]
    rows = size * count
    near = pl.BlockSpec(memory_space=pltpu.VMEM)
    return pl.pallas_call(
        functools.partial(score_kernel, count, offset),
        grid_spec=pltpu.PrefetchScalarGridSpec(
            num_scalar_prefetch=1,
            grid=(),
            in_specs=[near] * (count + 2),
            out_specs=near,
        ),
        out_shape=jax.ShapeDtypeStruct((8, rows), F32),
        compiler_params=pltpu.CompilerParams(vmem_limit_bytes=20 << 20),
        cost_estimate=pl.CostEstimate(
            flops=4 * rows * width * cols,
            bytes_accessed=2 * width * (2 * cols + rows),
            transcendentals=2 * rows * cols,
        ),
        name="score",
    )(bases, *pieces, vocabulary, target)


def per_device(
    embedded,
    states,
    w_query,
    w_key,
    w_value,
    w_output_gate,
    w_beta,
    w_decay,
    decay_rate,
    decay_bias,
    head_gain,
    input_gain,
    w_out,
    final_gain,
    lm_head,
    targets,
    active,
):
    steps, group, width = embedded.shape
    cols = lm_head.shape[1]
    me = lax.axis_index(AXES).astype(jnp.int32)
    core = lax.axis_index("c").astype(jnp.int32)
    batch = lax.axis_index(BATCH).astype(jnp.int32)
    head = lax.axis_index(HEAD).astype(jnp.int32)
    send = functools.partial(lax.ppermute, axis_name=AXES)
    far_head = send(lm_head, perm=OTHER_CORE)

    spot = jnp.stack([batch, head, core])
    give, keep = front(
        spot,
        decay_rate,
        decay_bias,
        embedded,
        states,
        w_query,
        w_key,
        w_value,
        w_output_gate,
        w_beta.T,
        w_decay.T,
        w_out,
        input_gain[None],
        head_gain[None],
        active.T,
    )
    block = keep.shape[0]
    table = sources()
    order = lax.dynamic_index_in_dim(jnp.asarray(table), me, 0, keepdims=False)
    inverse = lax.dynamic_index_in_dim(
        jnp.asarray(np.argsort(table, axis=1).astype(np.int32)), me, 0, keepdims=False
    )
    pair = (keep + send(give, perm=OTHER_CORE).astype(F32)).astype(BF16)
    bases = jnp.stack([me * cols, (me ^ GROUPS) * cols])
    pair, order, inverse, bases = lax.optimization_barrier((pair, order, inverse, bases))
    wanted = lax.dynamic_slice_in_dim(targets.T, core * (steps // 2), steps // 2, 0)
    wanted = jnp.take(wanted.reshape(steps // 2, GROUPS, group), order, axis=1)
    wanted = wanted.transpose(1, 0, 2).reshape(GROUPS * block, 1)
    from_low = send(pair, perm=OTHER_LOW)
    from_low, wanted, inverse = lax.optimization_barrier((from_low, wanted, inverse))
    summed = pair.astype(F32) + from_low.astype(F32)
    mine = lax.dynamic_slice_in_dim(embedded, core * (steps // 2), steps // 2, 0)
    y = mine.reshape(-1, width).astype(F32) + summed
    hidden = (
        y * lax.rsqrt(jnp.mean(y * y, axis=-1, keepdims=True) + EPS) * final_gain
    ).astype(BF16)

    both = jnp.concatenate([hidden, send(hidden, perm=OTHER_HIGH)], 0)
    near = jnp.concatenate([both] + [send(both, perm=p) for p in NEAR], 0)
    size = near.shape[0]
    forth, back = send(near, perm=FAR[0]), send(near, perm=FAR[1])
    far_head, near = lax.optimization_barrier((far_head, near))
    vocabulary = bring_in(lm_head, far_head)
    first = score(bases, [near], vocabulary, wanted, 0)
    forth, first = lax.optimization_barrier((forth, first))
    halves = [send(forth[: size // 2], perm=FAR[0])]
    back, first = lax.optimization_barrier((back, first))
    halves.append(send(back[size // 2 :], perm=FAR[1]))
    middle = score(bases, [forth, back], vocabulary, wanted, size)
    wanted, middle = lax.optimization_barrier((wanted, middle))
    stats = [first, middle, score(bases, halves, vocabulary, wanted, 3 * size)]
    stats = [part[:2] for part in stats]
    stats = jnp.concatenate(stats, 1).reshape(2, GROUPS, block).transpose(1, 0, 2)
    stats = jnp.take(stats.reshape(GROUPS, 2 * block), inverse, axis=0)
    stats = jnp.broadcast_to(stats[None], (4, GROUPS, 2 * block)).reshape(DEVICES, 2 * block)
    stats = lax.all_to_all(stats, AXES, 0, 0, tiled=True)
    stats = jnp.sum(stats.reshape(2, 2, GROUPS, 2, steps // 2, group), axis=(0, 2))
    total, picked = stats[:, 0].reshape(steps, group), stats[:, 1].reshape(steps, group)
    marks = lax.dynamic_slice_in_dim(active.T, batch * group, group, 1)
    return jnp.where(marks > 0, picked - jnp.log(total), 0.0).T


def solution(mesh):
    finer = Mesh(mesh.devices.reshape(SIZES), AXES)
    return jax.shard_map(
        per_device,
        mesh=finer,
        in_specs=(
            P(None, BATCH, None),
            P(BATCH, HEAD, None, None),
            P(None, HEAD),
            P(None, HEAD),
            P(None, HEAD),
            P(None, HEAD),
            P(None, HEAD),
            P(None, HEAD),
            P(),
            P(),
            P(),
            P(),
            P(HEAD, None),
            P(),
            P(None, HEAD + BATCH),
            P(),
            P(),
        ),
        out_specs=P(BATCH, None),
        check_vma=False,
    )
```

```python
import functools

import jax
import jax.numpy as jnp
import numpy as np
from jax import lax
from jax.experimental import pallas as pl
from jax.experimental.pallas import tpu as pltpu
from jax.sharding import Mesh
from jax.sharding import PartitionSpec as P

DK = 128
DV = 128
EPS = 1e-06
AXES = ("xl", "c", "y", "z", "xh")
SIZES = (2, 2, 4, 4, 2)
HEAD = ("xl", "c")
BATCH = ("y", "z", "xh")
DEVICES = 128
GROUPS = 32
F32 = jnp.float32
BF16 = jnp.bfloat16


def route(move):
    pairs = []
    for source in range(DEVICES):
        spot = [int(i) for i in np.unravel_index(source, SIZES)]
        pairs.append((source, int(np.ravel_multi_index(move(*spot), SIZES))))
    return pairs


def shift(first, second, hops):
    def move(xl, c, y, z, xh):
        if (first, second)[c] == "y":
            return (xl, c, (y + hops) % 4, z, xh)
        return (xl, c, y, (z + hops) % 4, xh)

    return route(move)


OTHER_CORE = route(lambda xl, c, y, z, xh: (xl, 1 - c, y, z, xh))
OTHER_LOW = route(lambda xl, c, y, z, xh: (1 - xl, c, y, z, xh))
OTHER_HIGH = route(lambda xl, c, y, z, xh: (xl, c, y, z, 1 - xh))
NEAR = [shift("y", "z", k) for k in (1, 3, 2)]
FAR = [shift("z", "y", k) for k in (1, 3, 2)]


def sources():
    held = [[d % GROUPS] for d in range(DEVICES)]
    for stage in ([OTHER_HIGH], NEAR, FAR):
        grown = [list(h) for h in held]
        for pairs in stage:
            for source, target in pairs:
                grown[target].extend(held[source])
        held = grown
    return np.array(held, np.int32)


def front_kernel(
    spot,
    rate,
    offset,
    embedded,
    states,
    w_query,
    w_key,
    w_value,
    w_gate,
    w_beta,
    w_decay,
    w_out,
    input_gain,
    head_gain,
    active,
    give,
    keep,
    normed,
    kq,
    reads,
    beta_all,
    decay_all,
    marks,
    mixed,
    total,
):
    step = pl.program_id(0)
    steps, group, width = embedded.shape
    rows = steps * group

    def contract_last(a, b):
        return lax.dot_general(a, b, (((1,), (1,)), ((), ())), preferred_element_type=F32)

    @pl.when(step == 0)
    def _():
        for t in range(steps):
            e = embedded[t].astype(F32)
            scale = lax.rsqrt(jnp.mean(e * e, axis=-1, keepdims=True) + EPS)
            normed[t * group : (t + 1) * group, :] = (e * scale * input_gain[...]).astype(BF16)
        n = normed[...]
        beta_raw = contract_last(n, w_beta[...]).astype(BF16).astype(F32)
        decay_raw = contract_last(n, w_decay[...]).astype(BF16).astype(F32)
        for h in range(w_beta.shape[0]):
            b = jnp.broadcast_to(beta_raw[:, h : h + 1], (rows, DV))
            d = jnp.broadcast_to(decay_raw[:, h : h + 1], (rows, DV))
            at = spot[1] * w_beta.shape[0] + h
            beta_all[h] = jax.nn.sigmoid(b)
            decay_all[h] = jnp.exp(-rate[at] * jax.nn.softplus(d + offset[at]))
        requests = active.shape[1]
        here = lax.broadcasted_iota(jnp.int32, (group, requests), 1) == (
            spot[0] * group + lax.broadcasted_iota(jnp.int32, (group, requests), 0)
        )
        for t in range(steps):
            line = jnp.broadcast_to(active[t : t + 1, :].astype(F32), (group, requests))
            column = jnp.sum(jnp.where(here, line, 0.0), axis=1, keepdims=True)
            marks[t] = jnp.broadcast_to(column, (group, DV))

    n = normed[...]

    def project(weight):
        return jnp.dot(n, weight[...], preferred_element_type=F32).astype(BF16).astype(F32)

    def unit(x):
        return x * lax.rsqrt(jnp.sum(x * x, axis=-1, keepdims=True) + EPS)

    kq[:rows, :] = unit(project(w_key))
    kq[rows:, :] = unit(project(w_query)) * DK ** (-0.5)
    value = project(w_value)
    gate = project(w_gate)
    k = [kq[t * group : (t + 1) * group, :] for t in range(steps)]
    q = [kq[rows + t * group : rows + (t + 1) * group, :] for t in range(steps)]

    def inner(a, b):
        return jnp.broadcast_to(jnp.sum(a * b, axis=-1, keepdims=True), (group, DV))

    kk = {(t, i): inner(k[t], k[i]) for t in range(steps) for i in range(t)}
    qk = {(t, i): inner(q[t], k[i]) for t in range(steps) for i in range(t + 1)}
    for r in range(group):
        lines = kq[pl.ds(r, 2 * steps, stride=group), :]
        high = lines.astype(BF16).astype(F32)
        both = jnp.concatenate([high, lines - high], axis=0).astype(BF16)
        for h in range(2):
            got = jnp.dot(both, states[r, h], preferred_element_type=F32)
            reads[h, pl.ds(r, 2 * steps, stride=group), :] = got[: 2 * steps] + got[2 * steps :]
    for h in range(2):
        head = 2 * step + h
        coefficient = []
        update = []
        for t in range(steps):
            at = slice(t * group, (t + 1) * group)
            decay = decay_all[head, at, :]
            beta = beta_all[head, at, :]
            mark = marks[t] > 0
            of_key = reads[h, at, :]
            of_query = reads[h, rows + t * group : rows + (t + 1) * group, :]
            if t > 0:
                of_key = start * of_key
                of_query = start * of_query
            for i in range(t):
                of_key = of_key + coefficient[i] * kk[t, i] * update[i]
                of_query = of_query + coefficient[i] * qk[t, i] * update[i]
            u = beta * (value[at, h * DV : (h + 1) * DV] - decay * of_key)
            readout = decay * of_query + qk[t, t] * u
            faded = jnp.where(mark, decay, 1.0)
            start = faded if t == 0 else start * faded
            coefficient = [old * faded for old in coefficient] + [jnp.where(mark, 1.0, 0.0)]
            update.append(u)
            scale = lax.rsqrt(jnp.mean(readout * readout, axis=-1, keepdims=True) + EPS)
            g = gate[at, h * DV : (h + 1) * DV]
            mixed[at, h * DV : (h + 1) * DV] = (
                readout * scale * head_gain[...] * (g * jax.nn.sigmoid(g))
            ).astype(BF16)
    part = jnp.dot(mixed[...], w_out[...], preferred_element_type=F32)

    @pl.when(step == 0)
    def _():
        total[...] = part

    @pl.when(step > 0)
    def _():
        total[...] += part

    @pl.when(step == pl.num_programs(0) - 1)
    def _():
        half = rows // 2
        c = spot[2]
        keep[...] = total[pl.ds(pl.multiple_of(c * half, half), half), :]
        give[...] = total[pl.ds(pl.multiple_of((1 - c) * half, half), half), :].astype(BF16)


def front(spot, rate, offset, embedded, states, wq, wk, wv, wg, wb, wd, wo, ig, hg, active):
    steps, group, width = embedded.shape
    rows, heads = steps * group, states.shape[1]
    key_heads = heads // 2
    whole = lambda *shape: pl.BlockSpec(shape, lambda j, *_: (0,) * len(shape))
    across = lambda cols: pl.BlockSpec((width, cols), lambda j, *_: (0, j))
    return pl.pallas_call(
        front_kernel,
        grid_spec=pltpu.PrefetchScalarGridSpec(
            num_scalar_prefetch=3,
            grid=(key_heads,),
            in_specs=[
                whole(steps, group, width),
                pl.BlockSpec((group, 2, DK, DV), lambda j, *_: (0, j, 0, 0)),
                across(DK),
                across(DK),
                across(2 * DV),
                across(2 * DV),
                whole(heads, width),
                whole(heads, width),
                pl.BlockSpec((2 * DV, width), lambda j, *_: (j, 0)),
                whole(1, width),
                whole(1, DV),
                whole(*active.shape),
            ],
            out_specs=[whole(rows // 2, width), whole(rows // 2, width)],
            scratch_shapes=[
                pltpu.VMEM((rows, width), BF16),
                pltpu.VMEM((2 * rows, DK), F32),
                pltpu.VMEM((2, 2 * rows, DV), F32),
                pltpu.VMEM((heads, rows, DV), F32),
                pltpu.VMEM((heads, rows, DV), F32),
                pltpu.VMEM((steps, group, DV), F32),
                pltpu.VMEM((rows, 2 * DV), BF16),
                pltpu.VMEM((rows, width), F32),
            ],
        ),
        out_shape=[
            jax.ShapeDtypeStruct((rows // 2, width), BF16),
            jax.ShapeDtypeStruct((rows // 2, width), F32),
        ],
        compiler_params=pltpu.CompilerParams(
            dimension_semantics=("arbitrary",), vmem_limit_bytes=60 << 20
        ),
        cost_estimate=pl.CostEstimate(
            flops=2 * rows * width * 4096, bytes_accessed=21 << 20, transcendentals=0
        ),
        name="front",
    )(spot, rate, offset, embedded, states, wq, wk, wv, wg, wb, wd, wo, ig, hg, active)


TILE = 512


def score_kernel(count, offset, bases, *refs):
    parts, (vocabulary, target, stats) = refs[:count], refs[count:]
    cols = vocabulary.shape[2]
    pieces = [
        jnp.concatenate([parts[i][...], parts[i + 1][...]], axis=0) for i in range(0, count, 2)
    ]
    size = pieces[0].shape[0]
    for p, piece in enumerate(pieces):
        at = slice(p * size, (p + 1) * size)
        lane = lax.broadcasted_iota(jnp.int32, (size, 128), 1)
        want = target[:, offset + p * size : offset + (p + 1) * size]
        want = jnp.broadcast_to(want, (128, size)).T - lane
        running = jnp.zeros((size, 128), F32)
        found = jnp.zeros((size, 128), F32)
        for start in range(0, cols, TILE):
            for which in range(2):
                logits = jnp.dot(
                    piece, vocabulary[which, :, start : start + TILE], preferred_element_type=F32
                )
                left = want - (bases[which] + start)
                for s in range(0, TILE, 128):
                    part = logits[:, s : s + 128]
                    running = running + jnp.exp(part)
                    found = found + jnp.where(left == s, part, 0.0)
        sums = jnp.sum(running, axis=1, keepdims=True)
        hits = jnp.sum(found, axis=1, keepdims=True)
        stats[:, at] = jnp.where(lane == 0, sums, hits).T[:8, :]


def gather_kernel(own, other, both, sems):
    copies = [
        pltpu.make_async_copy(source, both.at[i], sems.at[i])
        for i, source in enumerate((own, other))
    ]
    for copy in copies:
        copy.start()
    for copy in copies:
        copy.wait()


def bring_in(own, other):
    return pl.pallas_call(
        gather_kernel,
        in_specs=[pl.BlockSpec(memory_space=pltpu.HBM)] * 2,
        out_specs=pl.BlockSpec(memory_space=pltpu.VMEM),
        scratch_shapes=[pltpu.SemaphoreType.DMA((2,))],
        out_shape=jax.ShapeDtypeStruct((2, *own.shape), own.dtype),
        compiler_params=pltpu.CompilerParams(vmem_limit_bytes=12 << 20),
        cost_estimate=pl.CostEstimate(
            flops=0, bytes_accessed=4 * own.size, transcendentals=0
        ),
        name="bring_in",
    )(own, other)


def score(bases, pieces, vocabulary, target, offset):
    size, width = pieces[0].shape
    count, cols = len(pieces), vocabulary.shape[2]
    rows = size * count
    near = pl.BlockSpec(memory_space=pltpu.VMEM)
    return pl.pallas_call(
        functools.partial(score_kernel, count, offset),
        grid_spec=pltpu.PrefetchScalarGridSpec(
            num_scalar_prefetch=1,
            grid=(),
            in_specs=[near] * (count + 2),
            out_specs=near,
        ),
        out_shape=jax.ShapeDtypeStruct((8, rows), F32),
        compiler_params=pltpu.CompilerParams(vmem_limit_bytes=20 << 20),
        cost_estimate=pl.CostEstimate(
            flops=4 * rows * width * cols,
            bytes_accessed=2 * width * (2 * cols + rows),
            transcendentals=2 * rows * cols,
        ),
        name="score",
    )(bases, *pieces, vocabulary, target)


def per_device(
    embedded,
    states,
    w_query,
    w_key,
    w_value,
    w_output_gate,
    w_beta,
    w_decay,
    decay_rate,
    decay_bias,
    head_gain,
    input_gain,
    w_out,
    final_gain,
    lm_head,
    targets,
    active,
):
    steps, group, width = embedded.shape
    cols = lm_head.shape[1]
    me = lax.axis_index(AXES).astype(jnp.int32)
    core = lax.axis_index("c").astype(jnp.int32)
    batch = lax.axis_index(BATCH).astype(jnp.int32)
    head = lax.axis_index(HEAD).astype(jnp.int32)
    send = functools.partial(lax.ppermute, axis_name=AXES)
    far_head = send(lm_head, perm=OTHER_CORE)

    spot = jnp.stack([batch, head, core])
    give, keep = front(
        spot,
        decay_rate,
        decay_bias,
        embedded,
        states,
        w_query,
        w_key,
        w_value,
        w_output_gate,
        w_beta.T,
        w_decay.T,
        w_out,
        input_gain[None],
        head_gain[None],
        active.T,
    )
    block = keep.shape[0]
    table = sources()
    order = lax.dynamic_index_in_dim(jnp.asarray(table), me, 0, keepdims=False)
    inverse = lax.dynamic_index_in_dim(
        jnp.asarray(np.argsort(table, axis=1).astype(np.int32)), me, 0, keepdims=False
    )
    pair = (keep + send(give, perm=OTHER_CORE).astype(F32)).astype(BF16)
    bases = jnp.stack([me * cols, (me ^ GROUPS) * cols])
    pair, order, inverse, bases = lax.optimization_barrier((pair, order, inverse, bases))
    wanted = lax.dynamic_slice_in_dim(targets.T, core * (steps // 2), steps // 2, 0)
    wanted = jnp.take(wanted.reshape(steps // 2, GROUPS, group), order, axis=1)
    wanted = wanted.transpose(1, 0, 2).reshape(1, GROUPS * block)
    from_low = send(pair, perm=OTHER_LOW)
    from_low, wanted, inverse = lax.optimization_barrier((from_low, wanted, inverse))
    summed = pair.astype(F32) + from_low.astype(F32)
    mine = lax.dynamic_slice_in_dim(embedded, core * (steps // 2), steps // 2, 0)
    y = mine.reshape(-1, width).astype(F32) + summed
    hidden = (
        y * lax.rsqrt(jnp.mean(y * y, axis=-1, keepdims=True) + EPS) * final_gain
    ).astype(BF16)

    both = jnp.concatenate([hidden, send(hidden, perm=OTHER_HIGH)], 0)
    ahead, behind, across = [send(both, perm=p) for p in NEAR]
    one, two = jnp.concatenate([both, ahead], 0), jnp.concatenate([behind, across], 0)
    size = one.shape[0]
    forth_one, back_two = send(one, perm=FAR[0]), send(two, perm=FAR[1])
    forth_two, back_one = send(two, perm=FAR[0]), send(one, perm=FAR[1])
    far_head, one = lax.optimization_barrier((far_head, one))
    vocabulary = bring_in(lm_head, far_head)
    vocabulary, forth_one, back_two = lax.optimization_barrier((vocabulary, forth_one, back_two))
    halves = [send(forth_one, perm=FAR[0]), send(back_two, perm=FAR[1])]
    first = score(bases, [one, two], vocabulary, wanted, 0)
    wanted, first = lax.optimization_barrier((wanted, first))
    middle = [forth_one, forth_two, back_one, back_two]
    middle = score(bases, middle, vocabulary, wanted, 2 * size)
    wanted, middle = lax.optimization_barrier((wanted, middle))
    stats = [first, middle, score(bases, halves, vocabulary, wanted, 6 * size)]
    stats = [part[:2] for part in stats]
    stats = jnp.concatenate(stats, 1).reshape(2, GROUPS, block).transpose(1, 0, 2)
    stats = jnp.take(stats.reshape(GROUPS, 2 * block), inverse, axis=0)
    stats = jnp.broadcast_to(stats[None], (4, GROUPS, 2 * block)).reshape(DEVICES, 2 * block)
    stats = lax.all_to_all(stats, AXES, 0, 0, tiled=True)
    stats = jnp.sum(stats.reshape(2, 2, GROUPS, 2, steps // 2, group), axis=(0, 2))
    total, picked = stats[:, 0].reshape(steps, group), stats[:, 1].reshape(steps, group)
    marks = lax.dynamic_slice_in_dim(active.T, batch * group, group, 1)
    return jnp.where(marks > 0, picked - jnp.log(total), 0.0).T


def solution(mesh):
    finer = Mesh(mesh.devices.reshape(SIZES), AXES)
    return jax.shard_map(
        per_device,
        mesh=finer,
        in_specs=(
            P(None, BATCH, None),
            P(BATCH, HEAD, None, None),
            P(None, HEAD),
            P(None, HEAD),
            P(None, HEAD),
            P(None, HEAD),
            P(None, HEAD),
            P(None, HEAD),
            P(),
            P(),
            P(),
            P(),
            P(HEAD, None),
            P(),
            P(None, HEAD + BATCH),
            P(),
            P(),
        ),
        out_specs=P(BATCH, None),
        check_vma=False,
    )
```

```python
import functools

import jax
import jax.numpy as jnp
import numpy as np
from jax import lax
from jax.experimental import pallas as pl
from jax.experimental.pallas import tpu as pltpu
from jax.sharding import Mesh
from jax.sharding import PartitionSpec as P

DK = 128
DV = 128
EPS = 1e-06
AXES = ("xl", "c", "y", "z", "xh")
SIZES = (2, 2, 4, 4, 2)
HEAD = ("xl", "c")
BATCH = ("y", "z", "xh")
DEVICES = 128
GROUPS = 32
F32 = jnp.float32
BF16 = jnp.bfloat16


def route(move):
    pairs = []
    for source in range(DEVICES):
        spot = [int(i) for i in np.unravel_index(source, SIZES)]
        pairs.append((source, int(np.ravel_multi_index(move(*spot), SIZES))))
    return pairs


def shift(first, second, hops):
    def move(xl, c, y, z, xh):
        if (first, second)[c] == "y":
            return (xl, c, (y + hops) % 4, z, xh)
        return (xl, c, y, (z + hops) % 4, xh)

    return route(move)


OTHER_CORE = route(lambda xl, c, y, z, xh: (xl, 1 - c, y, z, xh))
OTHER_LOW = route(lambda xl, c, y, z, xh: (1 - xl, c, y, z, xh))
OTHER_HIGH = route(lambda xl, c, y, z, xh: (xl, c, y, z, 1 - xh))
OTHER_BOTH = route(lambda xl, c, y, z, xh: (1 - xl, c, y, z, 1 - xh))
NEAR = [shift("y", "z", k) for k in (1, 3, 2)]
FAR = [shift("z", "y", k) for k in (1, 3, 2)]


def sources():
    held = [[d % GROUPS] for d in range(DEVICES)]
    for stage in ([OTHER_HIGH], NEAR, FAR):
        grown = [list(h) for h in held]
        for pairs in stage:
            for source, target in pairs:
                grown[target].extend(held[source])
        held = grown
    return np.array(held, np.int32)


def front_kernel(
    spot,
    rate,
    offset,
    embedded,
    states,
    w_query,
    w_key,
    w_value,
    w_gate,
    w_beta,
    w_decay,
    w_out,
    input_gain,
    head_gain,
    active,
    give,
    keep,
    normed,
    kq,
    reads,
    beta_all,
    decay_all,
    marks,
    mixed,
    total,
):
    step = pl.program_id(0)
    steps, group, width = embedded.shape
    rows = steps * group

    def contract_last(a, b):
        return lax.dot_general(a, b, (((1,), (1,)), ((), ())), preferred_element_type=F32)

    @pl.when(step == 0)
    def _():
        for t in range(steps):
            e = embedded[t].astype(F32)
            scale = lax.rsqrt(jnp.mean(e * e, axis=-1, keepdims=True) + EPS)
            normed[t * group : (t + 1) * group, :] = (e * scale * input_gain[...]).astype(BF16)
        n = normed[...]
        beta_raw = contract_last(n, w_beta[...]).astype(BF16).astype(F32)
        decay_raw = contract_last(n, w_decay[...]).astype(BF16).astype(F32)
        for h in range(w_beta.shape[0]):
            b = jnp.broadcast_to(beta_raw[:, h : h + 1], (rows, DV))
            d = jnp.broadcast_to(decay_raw[:, h : h + 1], (rows, DV))
            at = spot[1] * w_beta.shape[0] + h
            beta_all[h] = jax.nn.sigmoid(b)
            decay_all[h] = jnp.exp(-rate[at] * jax.nn.softplus(d + offset[at]))
        requests = active.shape[1]
        here = lax.broadcasted_iota(jnp.int32, (group, requests), 1) == (
            spot[0] * group + lax.broadcasted_iota(jnp.int32, (group, requests), 0)
        )
        for t in range(steps):
            line = jnp.broadcast_to(active[t : t + 1, :].astype(F32), (group, requests))
            column = jnp.sum(jnp.where(here, line, 0.0), axis=1, keepdims=True)
            marks[t] = jnp.broadcast_to(column, (group, DV))

    n = normed[...]

    def project(weight):
        return jnp.dot(n, weight[...], preferred_element_type=F32).astype(BF16).astype(F32)

    def unit(x):
        return x * lax.rsqrt(jnp.sum(x * x, axis=-1, keepdims=True) + EPS)

    kq[:rows, :] = unit(project(w_key))
    kq[rows:, :] = unit(project(w_query)) * DK ** (-0.5)
    value = project(w_value)
    gate = project(w_gate)
    k = [kq[t * group : (t + 1) * group, :] for t in range(steps)]
    q = [kq[rows + t * group : rows + (t + 1) * group, :] for t in range(steps)]

    def inner(a, b):
        return jnp.broadcast_to(jnp.sum(a * b, axis=-1, keepdims=True), (group, DV))

    kk = {(t, i): inner(k[t], k[i]) for t in range(steps) for i in range(t)}
    qk = {(t, i): inner(q[t], k[i]) for t in range(steps) for i in range(t + 1)}
    for r in range(group):
        lines = kq[pl.ds(r, 2 * steps, stride=group), :]
        high = lines.astype(BF16).astype(F32)
        both = jnp.concatenate([high, lines - high], axis=0).astype(BF16)
        for h in range(2):
            got = jnp.dot(both, states[r, h], preferred_element_type=F32)
            reads[h, pl.ds(r, 2 * steps, stride=group), :] = got[: 2 * steps] + got[2 * steps :]
    for h in range(2):
        head = 2 * step + h
        coefficient = []
        update = []
        for t in range(steps):
            at = slice(t * group, (t + 1) * group)
            decay = decay_all[head, at, :]
            beta = beta_all[head, at, :]
            mark = marks[t] > 0
            of_key = reads[h, at, :]
            of_query = reads[h, rows + t * group : rows + (t + 1) * group, :]
            if t > 0:
                of_key = start * of_key
                of_query = start * of_query
            for i in range(t):
                of_key = of_key + coefficient[i] * kk[t, i] * update[i]
                of_query = of_query + coefficient[i] * qk[t, i] * update[i]
            u = beta * (value[at, h * DV : (h + 1) * DV] - decay * of_key)
            readout = decay * of_query + qk[t, t] * u
            faded = jnp.where(mark, decay, 1.0)
            start = faded if t == 0 else start * faded
            coefficient = [old * faded for old in coefficient] + [jnp.where(mark, 1.0, 0.0)]
            update.append(u)
            scale = lax.rsqrt(jnp.mean(readout * readout, axis=-1, keepdims=True) + EPS)
            g = gate[at, h * DV : (h + 1) * DV]
            mixed[at, h * DV : (h + 1) * DV] = (
                readout * scale * head_gain[...] * (g * jax.nn.sigmoid(g))
            ).astype(BF16)
    part = jnp.dot(mixed[...], w_out[...], preferred_element_type=F32)

    @pl.when(step == 0)
    def _():
        total[...] = part

    @pl.when(step > 0)
    def _():
        total[...] += part

    @pl.when(step == pl.num_programs(0) - 1)
    def _():
        half = rows // 2
        c = spot[2]
        tokens = embedded[pl.ds(c * (steps // 2), steps // 2)].astype(F32).reshape(half, width)
        first = jnp.where(spot[3] == 0, 1.0, 0.0)
        keep[...] = total[pl.ds(pl.multiple_of(c * half, half), half), :] + tokens * first
        give[...] = total[pl.ds(pl.multiple_of((1 - c) * half, half), half), :].astype(BF16)


def front(spot, rate, offset, embedded, states, wq, wk, wv, wg, wb, wd, wo, ig, hg, active):
    steps, group, width = embedded.shape
    rows, heads = steps * group, states.shape[1]
    key_heads = heads // 2
    whole = lambda *shape: pl.BlockSpec(shape, lambda j, *_: (0,) * len(shape))
    across = lambda cols: pl.BlockSpec((width, cols), lambda j, *_: (0, j))
    return pl.pallas_call(
        front_kernel,
        grid_spec=pltpu.PrefetchScalarGridSpec(
            num_scalar_prefetch=3,
            grid=(key_heads,),
            in_specs=[
                whole(steps, group, width),
                pl.BlockSpec((group, 2, DK, DV), lambda j, *_: (0, j, 0, 0)),
                across(DK),
                across(DK),
                across(2 * DV),
                across(2 * DV),
                whole(heads, width),
                whole(heads, width),
                pl.BlockSpec((2 * DV, width), lambda j, *_: (j, 0)),
                whole(1, width),
                whole(1, DV),
                whole(*active.shape),
            ],
            out_specs=[whole(rows // 2, width), whole(rows // 2, width)],
            scratch_shapes=[
                pltpu.VMEM((rows, width), BF16),
                pltpu.VMEM((2 * rows, DK), F32),
                pltpu.VMEM((2, 2 * rows, DV), F32),
                pltpu.VMEM((heads, rows, DV), F32),
                pltpu.VMEM((heads, rows, DV), F32),
                pltpu.VMEM((steps, group, DV), F32),
                pltpu.VMEM((rows, 2 * DV), BF16),
                pltpu.VMEM((rows, width), F32),
            ],
        ),
        out_shape=[
            jax.ShapeDtypeStruct((rows // 2, width), BF16),
            jax.ShapeDtypeStruct((rows // 2, width), F32),
        ],
        compiler_params=pltpu.CompilerParams(
            dimension_semantics=("arbitrary",), vmem_limit_bytes=60 << 20
        ),
        cost_estimate=pl.CostEstimate(
            flops=2 * rows * width * 4096, bytes_accessed=21 << 20, transcendentals=0
        ),
        name="front",
    )(spot, rate, offset, embedded, states, wq, wk, wv, wg, wb, wd, wo, ig, hg, active)


TILE = 512


def score_kernel(count, offset, bases, *refs):
    parts, (vocabulary, target, stats) = refs[:count], refs[count:]
    cols = vocabulary.shape[2]
    pieces = [
        jnp.concatenate([parts[i][...], parts[i + 1][...]], axis=0) for i in range(0, count, 2)
    ]
    size = pieces[0].shape[0]
    for p, piece in enumerate(pieces):
        at = slice(p * size, (p + 1) * size)
        lane = lax.broadcasted_iota(jnp.int32, (size, 128), 1)
        want = target[:, offset + p * size : offset + (p + 1) * size]
        want = jnp.broadcast_to(want, (128, size)).T - lane
        running = jnp.zeros((size, 128), F32)
        found = jnp.zeros((size, 128), F32)
        for start in range(0, cols, TILE):
            for which in range(2):
                logits = jnp.dot(
                    piece, vocabulary[which, :, start : start + TILE], preferred_element_type=F32
                )
                left = want - (bases[which] + start)
                for s in range(0, TILE, 128):
                    part = logits[:, s : s + 128]
                    running = running + jnp.exp(part)
                    found = found + jnp.where(left == s, part, 0.0)
        sums = jnp.sum(running, axis=1, keepdims=True)
        hits = jnp.sum(found, axis=1, keepdims=True)
        stats[:, at] = jnp.where(lane == 0, sums, hits).T[:8, :]


def gather_kernel(own, other, both, sems):
    copies = [
        pltpu.make_async_copy(source, both.at[i], sems.at[i])
        for i, source in enumerate((own, other))
    ]
    for copy in copies:
        copy.start()
    for copy in copies:
        copy.wait()


def bring_in(own, other):
    return pl.pallas_call(
        gather_kernel,
        in_specs=[pl.BlockSpec(memory_space=pltpu.HBM)] * 2,
        out_specs=pl.BlockSpec(memory_space=pltpu.VMEM),
        scratch_shapes=[pltpu.SemaphoreType.DMA((2,))],
        out_shape=jax.ShapeDtypeStruct((2, *own.shape), own.dtype),
        compiler_params=pltpu.CompilerParams(vmem_limit_bytes=12 << 20),
        cost_estimate=pl.CostEstimate(
            flops=0, bytes_accessed=4 * own.size, transcendentals=0
        ),
        name="bring_in",
    )(own, other)


def score(bases, pieces, vocabulary, target, offset):
    size, width = pieces[0].shape
    count, cols = len(pieces), vocabulary.shape[2]
    rows = size * count
    near = pl.BlockSpec(memory_space=pltpu.VMEM)
    return pl.pallas_call(
        functools.partial(score_kernel, count, offset),
        grid_spec=pltpu.PrefetchScalarGridSpec(
            num_scalar_prefetch=1,
            grid=(),
            in_specs=[near] * (count + 2),
            out_specs=near,
        ),
        out_shape=jax.ShapeDtypeStruct((8, rows), F32),
        compiler_params=pltpu.CompilerParams(vmem_limit_bytes=20 << 20),
        cost_estimate=pl.CostEstimate(
            flops=4 * rows * width * cols,
            bytes_accessed=2 * width * (2 * cols + rows),
            transcendentals=2 * rows * cols,
        ),
        name="score",
    )(bases, *pieces, vocabulary, target)


def per_device(
    embedded,
    states,
    w_query,
    w_key,
    w_value,
    w_output_gate,
    w_beta,
    w_decay,
    decay_rate,
    decay_bias,
    head_gain,
    input_gain,
    w_out,
    final_gain,
    lm_head,
    targets,
    active,
):
    steps, group, width = embedded.shape
    cols = lm_head.shape[1]
    me = lax.axis_index(AXES).astype(jnp.int32)
    core = lax.axis_index("c").astype(jnp.int32)
    batch = lax.axis_index(BATCH).astype(jnp.int32)
    head = lax.axis_index(HEAD).astype(jnp.int32)
    send = functools.partial(lax.ppermute, axis_name=AXES)
    far_head = send(lm_head, perm=OTHER_CORE)

    spot = jnp.stack([batch, head, core, lax.axis_index("xl").astype(jnp.int32)])
    give, keep = front(
        spot,
        decay_rate,
        decay_bias,
        embedded,
        states,
        w_query,
        w_key,
        w_value,
        w_output_gate,
        w_beta.T,
        w_decay.T,
        w_out,
        input_gain[None],
        head_gain[None],
        active.T,
    )
    block = keep.shape[0]
    table = sources()
    order = lax.dynamic_index_in_dim(jnp.asarray(table), me, 0, keepdims=False)
    inverse = lax.dynamic_index_in_dim(
        jnp.asarray(np.argsort(table, axis=1).astype(np.int32)), me, 0, keepdims=False
    )
    pair = (keep + send(give, perm=OTHER_CORE).astype(F32)).astype(BF16)
    bases = jnp.stack([me * cols, (me ^ GROUPS) * cols])
    pair, order, inverse, bases = lax.optimization_barrier((pair, order, inverse, bases))
    wanted = lax.dynamic_slice_in_dim(targets.T, core * (steps // 2), steps // 2, 0)
    wanted = jnp.take(wanted.reshape(steps // 2, GROUPS, group), order, axis=1)
    wanted = wanted.transpose(1, 0, 2).reshape(1, GROUPS * block)
    low, corner, high = [send(pair, perm=p) for p in (OTHER_LOW, OTHER_BOTH, OTHER_HIGH)]
    low, wanted, inverse = lax.optimization_barrier((low, wanted, inverse))

    def finish(a, b):
        y = a.astype(F32) + b.astype(F32)
        scale = lax.rsqrt(jnp.mean(y * y, axis=-1, keepdims=True) + EPS)
        return (y * scale * final_gain).astype(BF16)

    both = jnp.concatenate([finish(pair, low), finish(high, corner)], 0)
    far_head, both = lax.optimization_barrier((far_head, both))
    vocabulary = bring_in(lm_head, far_head)
    ahead, behind, across = [send(both, perm=p) for p in NEAR]
    ahead, vocabulary = lax.optimization_barrier((ahead, vocabulary))
    one, two = jnp.concatenate([both, ahead], 0), jnp.concatenate([behind, across], 0)
    size = one.shape[0]
    forth_one, back_two = send(one, perm=FAR[0]), send(two, perm=FAR[1])
    forth_two, back_one = send(two, perm=FAR[0]), send(one, perm=FAR[1])
    halves = [send(forth_one, perm=FAR[0]), send(back_two, perm=FAR[1])]
    first = score(bases, [one, two], vocabulary, wanted, 0)
    wanted, first = lax.optimization_barrier((wanted, first))
    middle = [forth_one, forth_two, back_one, back_two]
    middle = score(bases, middle, vocabulary, wanted, 2 * size)
    wanted, middle = lax.optimization_barrier((wanted, middle))
    stats = [first, middle, score(bases, halves, vocabulary, wanted, 6 * size)]
    stats = [part[:2] for part in stats]
    stats = jnp.concatenate(stats, 1).reshape(2, GROUPS, block).transpose(1, 0, 2)
    stats = jnp.take(stats.reshape(GROUPS, 2 * block), inverse, axis=0)
    stats = jnp.broadcast_to(stats[None], (4, GROUPS, 2 * block)).reshape(DEVICES, 2 * block)
    stats = lax.all_to_all(stats, AXES, 0, 0, tiled=True)
    stats = jnp.sum(stats.reshape(2, 2, GROUPS, 2, steps // 2, group), axis=(0, 2))
    total, picked = stats[:, 0].reshape(steps, group), stats[:, 1].reshape(steps, group)
    marks = lax.dynamic_slice_in_dim(active.T, batch * group, group, 1)
    return jnp.where(marks > 0, picked - jnp.log(total), 0.0).T


def solution(mesh):
    finer = Mesh(mesh.devices.reshape(SIZES), AXES)
    return jax.shard_map(
        per_device,
        mesh=finer,
        in_specs=(
            P(None, BATCH, None),
            P(BATCH, HEAD, None, None),
            P(None, HEAD),
            P(None, HEAD),
            P(None, HEAD),
            P(None, HEAD),
            P(None, HEAD),
            P(None, HEAD),
            P(),
            P(),
            P(),
            P(),
            P(HEAD, None),
            P(),
            P(None, HEAD + BATCH),
            P(),
            P(),
        ),
        out_specs=P(BATCH, None),
        check_vma=False,
    )
```

```python
import functools

import jax
import jax.numpy as jnp
import numpy as np
from jax import lax
from jax.experimental import pallas as pl
from jax.experimental.pallas import tpu as pltpu
from jax.sharding import Mesh
from jax.sharding import PartitionSpec as P

DK = 128
DV = 128
EPS = 1e-06
AXES = ("xl", "c", "y", "z", "xh")
SIZES = (2, 2, 4, 4, 2)
HEAD = ("xl", "c")
BATCH = ("y", "z", "xh")
DEVICES = 128
GROUPS = 32
F32 = jnp.float32
BF16 = jnp.bfloat16


def route(move):
    pairs = []
    for source in range(DEVICES):
        spot = [int(i) for i in np.unravel_index(source, SIZES)]
        pairs.append((source, int(np.ravel_multi_index(move(*spot), SIZES))))
    return pairs


def shift(first, second, hops):
    def move(xl, c, y, z, xh):
        if (first, second)[c] == "y":
            return (xl, c, (y + hops) % 4, z, xh)
        return (xl, c, y, (z + hops) % 4, xh)

    return route(move)


OTHER_CORE = route(lambda xl, c, y, z, xh: (xl, 1 - c, y, z, xh))
OTHER_LOW = route(lambda xl, c, y, z, xh: (1 - xl, c, y, z, xh))
OTHER_HIGH = route(lambda xl, c, y, z, xh: (xl, c, y, z, 1 - xh))
OTHER_BOTH = route(lambda xl, c, y, z, xh: (1 - xl, c, y, z, 1 - xh))
NEAR = [shift("y", "z", k) for k in (1, 3, 2)]
FAR = [shift("z", "y", k) for k in (1, 3, 2)]


def sources():
    held = [[d % GROUPS] for d in range(DEVICES)]
    for stage in ([OTHER_HIGH], NEAR, FAR):
        grown = [list(h) for h in held]
        for pairs in stage:
            for source, target in pairs:
                grown[target].extend(held[source])
        held = grown
    landing = [*range(12), *range(20, 24), *range(12, 20), *range(24, 32)]
    return np.array(held, np.int32)[:, landing]


def position():
    xl, c, y, z, xh = [lax.axis_index(axis).astype(jnp.int32) for axis in AXES]
    return xl, c, xl * 2 + c, (y * 4 + z) * 2 + xh


def front_kernel(
    rate,
    offset,
    embedded,
    states,
    w_query,
    w_key,
    w_value,
    w_gate,
    w_beta,
    w_decay,
    w_out,
    input_gain,
    head_gain,
    active,
    give,
    keep,
    normed,
    kq,
    reads,
    beta_all,
    decay_all,
    marks,
    mixed,
    total,
):
    step = pl.program_id(0)
    steps, group, width = embedded.shape
    rows = steps * group
    low_x, core, head_group, batch_group = position()

    def contract_last(a, b):
        return lax.dot_general(a, b, (((1,), (1,)), ((), ())), preferred_element_type=F32)

    @pl.when(step == 0)
    def _():
        for t in range(steps):
            e = embedded[t].astype(F32)
            scale = lax.rsqrt(jnp.mean(e * e, axis=-1, keepdims=True) + EPS)
            normed[t * group : (t + 1) * group, :] = (e * scale * input_gain[...]).astype(BF16)
        n = normed[...]
        beta_raw = contract_last(n, w_beta[...]).astype(BF16).astype(F32)
        decay_raw = contract_last(n, w_decay[...]).astype(BF16).astype(F32)
        for h in range(w_beta.shape[0]):
            b = jnp.broadcast_to(beta_raw[:, h : h + 1], (rows, DV))
            d = jnp.broadcast_to(decay_raw[:, h : h + 1], (rows, DV))
            at = head_group * w_beta.shape[0] + h
            beta_all[h] = jax.nn.sigmoid(b)
            decay_all[h] = jnp.exp(-rate[at] * jax.nn.softplus(d + offset[at]))
        requests = active.shape[1]
        here = lax.broadcasted_iota(jnp.int32, (group, requests), 1) == (
            batch_group * group + lax.broadcasted_iota(jnp.int32, (group, requests), 0)
        )
        for t in range(steps):
            line = jnp.broadcast_to(active[t : t + 1, :].astype(F32), (group, requests))
            column = jnp.sum(jnp.where(here, line, 0.0), axis=1, keepdims=True)
            marks[t] = jnp.broadcast_to(column, (group, DV))

    n = normed[...]

    def project(weight):
        return jnp.dot(n, weight[...], preferred_element_type=F32).astype(BF16).astype(F32)

    def unit(x):
        return x * lax.rsqrt(jnp.sum(x * x, axis=-1, keepdims=True) + EPS)

    kq[:rows, :] = unit(project(w_key))
    kq[rows:, :] = unit(project(w_query)) * DK ** (-0.5)
    value = project(w_value)
    gate = project(w_gate)
    k = [kq[t * group : (t + 1) * group, :] for t in range(steps)]
    q = [kq[rows + t * group : rows + (t + 1) * group, :] for t in range(steps)]

    def inner(a, b):
        return jnp.broadcast_to(jnp.sum(a * b, axis=-1, keepdims=True), (group, DV))

    kk = {(t, i): inner(k[t], k[i]) for t in range(steps) for i in range(t)}
    qk = {(t, i): inner(q[t], k[i]) for t in range(steps) for i in range(t + 1)}
    for r in range(group):
        lines = kq[pl.ds(r, 2 * steps, stride=group), :]
        high = lines.astype(BF16).astype(F32)
        both = jnp.concatenate([high, lines - high], axis=0).astype(BF16)
        for h in range(2):
            got = jnp.dot(both, states[r, h], preferred_element_type=F32)
            reads[h, pl.ds(r, 2 * steps, stride=group), :] = got[: 2 * steps] + got[2 * steps :]
    for h in range(2):
        head = 2 * step + h
        coefficient = []
        update = []
        for t in range(steps):
            at = slice(t * group, (t + 1) * group)
            decay = decay_all[head, at, :]
            beta = beta_all[head, at, :]
            mark = marks[t] > 0
            of_key = reads[h, at, :]
            of_query = reads[h, rows + t * group : rows + (t + 1) * group, :]
            if t > 0:
                of_key = start * of_key
                of_query = start * of_query
            for i in range(t):
                of_key = of_key + coefficient[i] * kk[t, i] * update[i]
                of_query = of_query + coefficient[i] * qk[t, i] * update[i]
            u = beta * (value[at, h * DV : (h + 1) * DV] - decay * of_key)
            readout = decay * of_query + qk[t, t] * u
            faded = jnp.where(mark, decay, 1.0)
            start = faded if t == 0 else start * faded
            coefficient = [old * faded for old in coefficient] + [jnp.where(mark, 1.0, 0.0)]
            update.append(u)
            scale = lax.rsqrt(jnp.mean(readout * readout, axis=-1, keepdims=True) + EPS)
            g = gate[at, h * DV : (h + 1) * DV]
            mixed[at, h * DV : (h + 1) * DV] = (
                readout * scale * head_gain[...] * (g * jax.nn.sigmoid(g))
            ).astype(BF16)
    part = jnp.dot(mixed[...], w_out[...], preferred_element_type=F32)

    @pl.when(step == 0)
    def _():
        total[...] = part

    @pl.when(step > 0)
    def _():
        total[...] += part

    @pl.when(step == pl.num_programs(0) - 1)
    def _():
        half = rows // 2
        c = core
        tokens = embedded[pl.ds(c * (steps // 2), steps // 2)].astype(F32).reshape(half, width)
        first = jnp.where(low_x == 0, 1.0, 0.0)
        keep[...] = total[pl.ds(pl.multiple_of(c * half, half), half), :] + tokens * first
        give[...] = total[pl.ds(pl.multiple_of((1 - c) * half, half), half), :].astype(BF16)


def front(rate, offset, embedded, states, wq, wk, wv, wg, wb, wd, wo, ig, hg, active):
    steps, group, width = embedded.shape
    rows, heads = steps * group, states.shape[1]
    key_heads = heads // 2
    whole = lambda *shape: pl.BlockSpec(shape, lambda j, *_: (0,) * len(shape))
    across = lambda cols: pl.BlockSpec((width, cols), lambda j, *_: (0, j))
    return pl.pallas_call(
        front_kernel,
        grid_spec=pltpu.PrefetchScalarGridSpec(
            num_scalar_prefetch=2,
            grid=(key_heads,),
            in_specs=[
                whole(steps, group, width),
                pl.BlockSpec((group, 2, DK, DV), lambda j, *_: (0, j, 0, 0)),
                across(DK),
                across(DK),
                across(2 * DV),
                across(2 * DV),
                whole(heads, width),
                whole(heads, width),
                pl.BlockSpec((2 * DV, width), lambda j, *_: (j, 0)),
                whole(1, width),
                whole(1, DV),
                whole(*active.shape),
            ],
            out_specs=[whole(rows // 2, width), whole(rows // 2, width)],
            scratch_shapes=[
                pltpu.VMEM((rows, width), BF16),
                pltpu.VMEM((2 * rows, DK), F32),
                pltpu.VMEM((2, 2 * rows, DV), F32),
                pltpu.VMEM((heads, rows, DV), F32),
                pltpu.VMEM((heads, rows, DV), F32),
                pltpu.VMEM((steps, group, DV), F32),
                pltpu.VMEM((rows, 2 * DV), BF16),
                pltpu.VMEM((rows, width), F32),
            ],
        ),
        out_shape=[
            jax.ShapeDtypeStruct((rows // 2, width), BF16),
            jax.ShapeDtypeStruct((rows // 2, width), F32),
        ],
        compiler_params=pltpu.CompilerParams(
            dimension_semantics=("arbitrary",), vmem_limit_bytes=60 << 20
        ),
        cost_estimate=pl.CostEstimate(
            flops=2 * rows * width * 4096, bytes_accessed=21 << 20, transcendentals=0
        ),
        name="front",
    )(rate, offset, embedded, states, wq, wk, wv, wg, wb, wd, wo, ig, hg, active)


TILE = 512


def score_block(parts, vocabulary, target, offset):
    piece = jnp.concatenate([part[...] for part in parts], axis=0)
    size, cols = piece.shape[0], vocabulary.shape[2]
    _, core, head_group, batch_group = position()
    base = (head_group * GROUPS + batch_group) * cols
    bases = (base, base + (1 - 2 * core) * GROUPS * cols)
    lane = lax.broadcasted_iota(jnp.int32, (size, 128), 1)
    want = jnp.broadcast_to(target[:, offset : offset + size], (128, size)).T - lane
    running = jnp.zeros((size, 128), F32)
    found = jnp.zeros((size, 128), F32)
    for start in range(0, cols, TILE):
        for which in range(2):
            logits = jnp.dot(
                piece, vocabulary[which, :, start : start + TILE], preferred_element_type=F32
            )
            left = want - (bases[which] + start)
            for s in range(0, TILE, 128):
                part = logits[:, s : s + 128]
                running = running + jnp.exp(part)
                found = found + jnp.where(left == s, part, 0.0)
    sums = jnp.sum(running, axis=1, keepdims=True)
    hits = jnp.sum(found, axis=1, keepdims=True)
    return jnp.where(lane == 0, sums, hits).T[:8, :]


def score_kernel(offset, one, two, vocabulary, target, stats):
    stats[...] = score_block((one, two), vocabulary, target, offset)


def last_score_kernel(offset, order, one, two, vocabulary, target, *refs):
    earlier, outgoing = refs[:-1], refs[-1]
    blocks = [part[...] for part in earlier] + [score_block((one, two), vocabulary, target, offset)]
    half = outgoing.shape[1] // 2
    at = 0
    for block in blocks:
        for s in range(0, block.shape[1], half):
            row = jnp.concatenate([block[0:1, s : s + half], block[1:2, s : s + half]], axis=1)
            for head in range(4):
                outgoing[pl.ds(order[at] + head * GROUPS, 1), :] = row
            at += 1


def score(parts, vocabulary, target, offset, earlier=(), order=None):
    size, width = parts[0].shape
    rows, cols = 2 * size, vocabulary.shape[2]
    near = pl.BlockSpec(memory_space=pltpu.VMEM)
    last = order is not None
    kernel = last_score_kernel if last else score_kernel
    shape = (DEVICES, 2 * rows * 4 // GROUPS) if last else (8, rows)
    return pl.pallas_call(
        functools.partial(kernel, offset),
        grid_spec=pltpu.PrefetchScalarGridSpec(
            num_scalar_prefetch=int(last),
            grid=(),
            in_specs=[near] * (4 + len(earlier)),
            out_specs=near,
        ),
        out_shape=jax.ShapeDtypeStruct(shape, F32),
        compiler_params=pltpu.CompilerParams(vmem_limit_bytes=20 << 20),
        cost_estimate=pl.CostEstimate(
            flops=4 * rows * width * cols,
            bytes_accessed=2 * width * (2 * cols + rows),
            transcendentals=2 * rows * cols,
        ),
        name="last_score" if last else "score",
    )(*([order] if last else []), *parts, vocabulary, target, *earlier)


def finish_kernel(incoming, marks, scores):
    block = GROUPS
    for core in range(2):
        total = sum(
            jnp.sum(incoming[(x * 2 + core) * block : (x * 2 + core + 1) * block, :], axis=0, keepdims=True)
            for x in range(2)
        )
        half = total.shape[1] // 2
        group = half // 2
        result = total[:, half:] - jnp.log(total[:, :half])
        for t in range(2):
            row = slice(core * 2 + t, core * 2 + t + 1)
            part = result[:, t * group : (t + 1) * group]
            scores[row, :] = jnp.where(marks[row, :] > 0, part, 0.0)


def finish_scores(incoming, marks):
    near = pl.BlockSpec(memory_space=pltpu.VMEM)
    return pl.pallas_call(
        finish_kernel,
        in_specs=[near, near],
        out_specs=near,
        out_shape=jax.ShapeDtypeStruct(marks.shape, F32),
        compiler_params=pltpu.CompilerParams(vmem_limit_bytes=4 << 20),
        name="finish",
    )(incoming, marks)


def gather_kernel(own, other, both, sems):
    copies = [
        pltpu.make_async_copy(source, both.at[i], sems.at[i])
        for i, source in enumerate((own, other))
    ]
    for copy in copies:
        copy.start()
    for copy in copies:
        copy.wait()


def bring_in(own, other):
    return pl.pallas_call(
        gather_kernel,
        in_specs=[pl.BlockSpec(memory_space=pltpu.HBM)] * 2,
        out_specs=pl.BlockSpec(memory_space=pltpu.VMEM),
        scratch_shapes=[pltpu.SemaphoreType.DMA((2,))],
        out_shape=jax.ShapeDtypeStruct((2, *own.shape), own.dtype),
        compiler_params=pltpu.CompilerParams(vmem_limit_bytes=12 << 20),
        cost_estimate=pl.CostEstimate(
            flops=0, bytes_accessed=4 * own.size, transcendentals=0
        ),
        name="bring_in",
    )(own, other)


def per_device(
    embedded,
    states,
    w_query,
    w_key,
    w_value,
    w_output_gate,
    w_beta,
    w_decay,
    decay_rate,
    decay_bias,
    head_gain,
    input_gain,
    w_out,
    final_gain,
    lm_head,
    targets,
    active,
):
    steps, group, width = embedded.shape
    me = lax.axis_index(AXES).astype(jnp.int32)
    core = lax.axis_index("c").astype(jnp.int32)
    batch = lax.axis_index(BATCH).astype(jnp.int32)
    send = functools.partial(lax.ppermute, axis_name=AXES)
    far_head = send(lm_head, perm=OTHER_CORE)

    give, keep = front(
        decay_rate,
        decay_bias,
        embedded,
        states,
        w_query,
        w_key,
        w_value,
        w_output_gate,
        w_beta.T,
        w_decay.T,
        w_out,
        input_gain[None],
        head_gain[None],
        active.T,
    )
    block = keep.shape[0]
    pair = (keep + send(give, perm=OTHER_CORE).astype(F32)).astype(BF16)
    pair, me, core, batch = lax.optimization_barrier((pair, me, core, batch))
    order = lax.dynamic_index_in_dim(jnp.asarray(sources()), me, 0, keepdims=False)
    wanted = lax.dynamic_slice_in_dim(targets.T, core * (steps // 2), steps // 2, 0)
    wanted = jnp.take(wanted.reshape(steps // 2, GROUPS, group), order, axis=1)
    wanted = wanted.transpose(1, 0, 2).reshape(1, GROUPS * block)
    marks = lax.dynamic_slice_in_dim(active.T, batch * group, group, 1)
    low, corner, high = [send(pair, perm=p) for p in (OTHER_LOW, OTHER_BOTH, OTHER_HIGH)]
    low, wanted, order, marks = lax.optimization_barrier((low, wanted, order, marks))

    def finish(a, b):
        y = a.astype(F32) + b.astype(F32)
        scale = lax.rsqrt(jnp.mean(y * y, axis=-1, keepdims=True) + EPS)
        return (y * scale * final_gain).astype(BF16)

    both = jnp.concatenate([finish(pair, low), finish(high, corner)], 0)
    far_head, both = lax.optimization_barrier((far_head, both))
    vocabulary = bring_in(lm_head, far_head)
    ahead, behind, across = [send(both, perm=p) for p in NEAR]
    ahead, vocabulary = lax.optimization_barrier((ahead, vocabulary))
    one, two = jnp.concatenate([both, ahead], 0), jnp.concatenate([behind, across], 0)
    size = one.shape[0]
    forth_one, back_two = send(one, perm=FAR[0]), send(two, perm=FAR[1])
    forth_two, back_one = send(two, perm=FAR[0]), send(one, perm=FAR[1])
    halves = [send(forth_one, perm=FAR[0]), send(back_two, perm=FAR[1])]
    stats = []
    arrivals = ((one, two), (forth_one, back_two), (forth_two, back_one))
    for i, parts in enumerate(arrivals):
        stats.append(score(parts, vocabulary, wanted, 2 * size * i))
        wanted, stats[i] = lax.optimization_barrier((wanted, stats[i]))
    outgoing = score(halves, vocabulary, wanted, 6 * size, stats, order)
    incoming = lax.all_to_all(outgoing, AXES, 0, 0, tiled=True)
    return finish_scores(incoming, marks).T


def solution(mesh):
    finer = Mesh(mesh.devices.reshape(SIZES), AXES)
    return jax.shard_map(
        per_device,
        mesh=finer,
        in_specs=(
            P(None, BATCH, None),
            P(BATCH, HEAD, None, None),
            P(None, HEAD),
            P(None, HEAD),
            P(None, HEAD),
            P(None, HEAD),
            P(None, HEAD),
            P(None, HEAD),
            P(),
            P(),
            P(),
            P(),
            P(HEAD, None),
            P(),
            P(None, HEAD + BATCH),
            P(),
            P(),
        ),
        out_specs=P(BATCH, None),
        check_vma=False,
    )
```

```python
import functools

import jax
import jax.numpy as jnp
import numpy as np
from jax import lax
from jax.experimental import pallas as pl
from jax.experimental.pallas import tpu as pltpu
from jax.sharding import Mesh
from jax.sharding import PartitionSpec as P

DK = 128
DV = 128
EPS = 1e-06
AXES = ("xl", "c", "y", "z", "xh")
SIZES = (2, 2, 4, 4, 2)
HEAD = ("xl", "c")
BATCH = ("y", "z", "xh")
DEVICES = 128
GROUPS = 32
F32 = jnp.float32
BF16 = jnp.bfloat16


def route(move):
    pairs = []
    for source in range(DEVICES):
        spot = [int(i) for i in np.unravel_index(source, SIZES)]
        pairs.append((source, int(np.ravel_multi_index(move(*spot), SIZES))))
    return pairs


def shift(first, second, hops):
    def move(xl, c, y, z, xh):
        if (first, second)[c] == "y":
            return (xl, c, (y + hops) % 4, z, xh)
        return (xl, c, y, (z + hops) % 4, xh)

    return route(move)


OTHER_CORE = route(lambda xl, c, y, z, xh: (xl, 1 - c, y, z, xh))
OTHER_LOW = route(lambda xl, c, y, z, xh: (1 - xl, c, y, z, xh))
OTHER_HIGH = route(lambda xl, c, y, z, xh: (xl, c, y, z, 1 - xh))
OTHER_BOTH = route(lambda xl, c, y, z, xh: (1 - xl, c, y, z, 1 - xh))
NEAR = [shift("y", "z", k) for k in (1, 3, 2)]
FAR = [shift("z", "y", k) for k in (1, 3, 2)]


def sources():
    held = [[d % GROUPS] for d in range(DEVICES)]
    for stage in ([OTHER_HIGH], NEAR, FAR):
        grown = [list(h) for h in held]
        for pairs in stage:
            for source, target in pairs:
                grown[target].extend(held[source])
        held = grown
    landing = [*range(12), *range(20, 24), *range(12, 20), *range(24, 32)]
    return np.array(held, np.int32)[:, landing]


def position():
    xl, c, y, z, xh = [lax.axis_index(axis).astype(jnp.int32) for axis in AXES]
    return xl, c, xl * 2 + c, (y * 4 + z) * 2 + xh


def front_kernel(
    rate,
    offset,
    embedded,
    states,
    w_query,
    w_key,
    w_value,
    w_gate,
    w_beta,
    w_decay,
    w_out,
    input_gain,
    head_gain,
    active,
    give,
    keep,
    normed,
    kq,
    reads,
    beta_all,
    decay_all,
    marks,
    mixed,
    total,
):
    step = pl.program_id(0)
    steps, group, width = embedded.shape
    rows = steps * group
    low_x, core, head_group, batch_group = position()

    def contract_last(a, b):
        return lax.dot_general(a, b, (((1,), (1,)), ((), ())), preferred_element_type=F32)

    @pl.when(step == 0)
    def _():
        for t in range(steps):
            e = embedded[t].astype(F32)
            scale = lax.rsqrt(jnp.mean(e * e, axis=-1, keepdims=True) + EPS)
            normed[t * group : (t + 1) * group, :] = (e * scale * input_gain[...]).astype(BF16)
        n = normed[...]
        beta_raw = contract_last(n, w_beta[...]).astype(BF16).astype(F32)
        decay_raw = contract_last(n, w_decay[...]).astype(BF16).astype(F32)
        for h in range(w_beta.shape[0]):
            b = jnp.broadcast_to(beta_raw[:, h : h + 1], (rows, DV))
            d = jnp.broadcast_to(decay_raw[:, h : h + 1], (rows, DV))
            at = head_group * w_beta.shape[0] + h
            beta_all[h] = jax.nn.sigmoid(b)
            decay_all[h] = jnp.exp(-rate[at] * jax.nn.softplus(d + offset[at]))
        requests = active.shape[1]
        here = lax.broadcasted_iota(jnp.int32, (group, requests), 1) == (
            batch_group * group + lax.broadcasted_iota(jnp.int32, (group, requests), 0)
        )
        for t in range(steps):
            line = jnp.broadcast_to(active[t : t + 1, :].astype(F32), (group, requests))
            column = jnp.sum(jnp.where(here, line, 0.0), axis=1, keepdims=True)
            marks[t] = jnp.broadcast_to(column, (group, DV))

    n = normed[...]

    def project(weight):
        return jnp.dot(n, weight[...], preferred_element_type=F32).astype(BF16).astype(F32)

    def unit(x):
        return x * lax.rsqrt(jnp.sum(x * x, axis=-1, keepdims=True) + EPS)

    kq[:rows, :] = unit(project(w_key))
    kq[rows:, :] = unit(project(w_query)) * DK ** (-0.5)
    value = project(w_value)
    gate = project(w_gate)
    k = [kq[t * group : (t + 1) * group, :] for t in range(steps)]
    q = [kq[rows + t * group : rows + (t + 1) * group, :] for t in range(steps)]

    def inner(a, b):
        return jnp.broadcast_to(jnp.sum(a * b, axis=-1, keepdims=True), (group, DV))

    kk = {(t, i): inner(k[t], k[i]) for t in range(steps) for i in range(t)}
    qk = {(t, i): inner(q[t], k[i]) for t in range(steps) for i in range(t + 1)}
    for r in range(group):
        lines = kq[pl.ds(r, 2 * steps, stride=group), :]
        high = lines.astype(BF16).astype(F32)
        both = jnp.concatenate([high, lines - high], axis=0).astype(BF16)
        for h in range(2):
            got = jnp.dot(both, states[r, h], preferred_element_type=F32)
            reads[h, pl.ds(r, 2 * steps, stride=group), :] = got[: 2 * steps] + got[2 * steps :]
    for h in range(2):
        head = 2 * step + h
        coefficient = []
        update = []
        for t in range(steps):
            at = slice(t * group, (t + 1) * group)
            decay = decay_all[head, at, :]
            beta = beta_all[head, at, :]
            mark = marks[t] > 0
            of_key = reads[h, at, :]
            of_query = reads[h, rows + t * group : rows + (t + 1) * group, :]
            if t > 0:
                of_key = start * of_key
                of_query = start * of_query
            for i in range(t):
                of_key = of_key + coefficient[i] * kk[t, i] * update[i]
                of_query = of_query + coefficient[i] * qk[t, i] * update[i]
            u = beta * (value[at, h * DV : (h + 1) * DV] - decay * of_key)
            readout = decay * of_query + qk[t, t] * u
            faded = jnp.where(mark, decay, 1.0)
            start = faded if t == 0 else start * faded
            coefficient = [old * faded for old in coefficient] + [jnp.where(mark, 1.0, 0.0)]
            update.append(u)
            scale = lax.rsqrt(jnp.mean(readout * readout, axis=-1, keepdims=True) + EPS)
            g = gate[at, h * DV : (h + 1) * DV]
            mixed[at, h * DV : (h + 1) * DV] = (
                readout * scale * head_gain[...] * (g * jax.nn.sigmoid(g))
            ).astype(BF16)
    part = jnp.dot(mixed[...], w_out[...], preferred_element_type=F32)

    @pl.when(step == 0)
    def _():
        total[...] = part

    @pl.when(step > 0)
    def _():
        total[...] += part

    @pl.when(step == pl.num_programs(0) - 1)
    def _():
        half = rows // 2
        c = core
        tokens = embedded[pl.ds(c * (steps // 2), steps // 2)].astype(F32).reshape(half, width)
        first = jnp.where(low_x == 0, 1.0, 0.0)
        keep[...] = total[pl.ds(pl.multiple_of(c * half, half), half), :] + tokens * first
        give[...] = total[pl.ds(pl.multiple_of((1 - c) * half, half), half), :].astype(BF16)


def front(rate, offset, embedded, states, wq, wk, wv, wg, wb, wd, wo, ig, hg, active):
    steps, group, width = embedded.shape
    rows, heads = steps * group, states.shape[1]
    key_heads = heads // 2
    whole = lambda *shape: pl.BlockSpec(shape, lambda j, *_: (0,) * len(shape))
    across = lambda cols: pl.BlockSpec((width, cols), lambda j, *_: (0, j))
    return pl.pallas_call(
        front_kernel,
        grid_spec=pltpu.PrefetchScalarGridSpec(
            num_scalar_prefetch=2,
            grid=(key_heads,),
            in_specs=[
                whole(steps, group, width),
                pl.BlockSpec((group, 2, DK, DV), lambda j, *_: (0, j, 0, 0)),
                across(DK),
                across(DK),
                across(2 * DV),
                across(2 * DV),
                whole(heads, width),
                whole(heads, width),
                pl.BlockSpec((2 * DV, width), lambda j, *_: (j, 0)),
                whole(1, width),
                whole(1, DV),
                whole(*active.shape),
            ],
            out_specs=[whole(rows // 2, width), whole(rows // 2, width)],
            scratch_shapes=[
                pltpu.VMEM((rows, width), BF16),
                pltpu.VMEM((2 * rows, DK), F32),
                pltpu.VMEM((2, 2 * rows, DV), F32),
                pltpu.VMEM((heads, rows, DV), F32),
                pltpu.VMEM((heads, rows, DV), F32),
                pltpu.VMEM((steps, group, DV), F32),
                pltpu.VMEM((rows, 2 * DV), BF16),
                pltpu.VMEM((rows, width), F32),
            ],
        ),
        out_shape=[
            jax.ShapeDtypeStruct((rows // 2, width), BF16),
            jax.ShapeDtypeStruct((rows // 2, width), F32),
        ],
        compiler_params=pltpu.CompilerParams(
            dimension_semantics=("arbitrary",), vmem_limit_bytes=60 << 20
        ),
        cost_estimate=pl.CostEstimate(
            flops=2 * rows * width * 4096, bytes_accessed=21 << 20, transcendentals=0
        ),
        name="front",
    )(rate, offset, embedded, states, wq, wk, wv, wg, wb, wd, wo, ig, hg, active)


TILE = 512


def score_block(parts, own, other, target, offset):
    piece = jnp.concatenate([part[...] for part in parts], axis=0)
    size, cols = piece.shape[0], own.shape[1]
    _, core, head_group, batch_group = position()
    base = (head_group * GROUPS + batch_group) * cols
    bases = (base, base + (1 - 2 * core) * GROUPS * cols)
    lane = lax.broadcasted_iota(jnp.int32, (size, 128), 1)
    want = jnp.broadcast_to(target[:, offset : offset + size], (128, size)).T - lane
    running = jnp.zeros((size, 128), F32)
    found = jnp.zeros((size, 128), F32)
    for start in range(0, cols, TILE):
        for base, weight in zip(bases, (own, other)):
            logits = jnp.dot(piece, weight[:, start : start + TILE], preferred_element_type=F32)
            left = want - (base + start)
            for s in range(0, TILE, 128):
                part = logits[:, s : s + 128]
                running = running + jnp.exp(part)
                found = found + jnp.where(left == s, part, 0.0)
    sums = jnp.sum(running, axis=1, keepdims=True)
    hits = jnp.sum(found, axis=1, keepdims=True)
    return jnp.where(lane == 0, sums, hits).T[:8, :]


def score_kernel(offset, one, two, own, other, target, stats):
    stats[...] = score_block((one, two), own, other, target, offset)


def last_score_kernel(offset, order, one, two, own, other, target, *refs):
    earlier, outgoing = refs[:-1], refs[-1]
    blocks = [part[...] for part in earlier]
    blocks.append(score_block((one, two), own, other, target, offset))
    half = outgoing.shape[1] // 2
    at = 0
    for block in blocks:
        for s in range(0, block.shape[1], half):
            row = jnp.concatenate([block[0:1, s : s + half], block[1:2, s : s + half]], axis=1)
            for head in range(4):
                outgoing[pl.ds(order[at] + head * GROUPS, 1), :] = row
            at += 1


def score(parts, own, other, target, offset, earlier=(), order=None):
    size, width = parts[0].shape
    rows, cols = 2 * size, own.shape[1]
    near = pl.BlockSpec(memory_space=pltpu.VMEM)
    last = order is not None
    kernel = last_score_kernel if last else score_kernel
    shape = (DEVICES, 2 * rows * 4 // GROUPS) if last else (8, rows)
    return pl.pallas_call(
        functools.partial(kernel, offset),
        grid_spec=pltpu.PrefetchScalarGridSpec(
            num_scalar_prefetch=int(last),
            grid=(),
            in_specs=[near] * (5 + len(earlier)),
            out_specs=near,
        ),
        out_shape=jax.ShapeDtypeStruct(shape, F32),
        compiler_params=pltpu.CompilerParams(vmem_limit_bytes=20 << 20),
        cost_estimate=pl.CostEstimate(
            flops=4 * rows * width * cols,
            bytes_accessed=2 * width * (2 * cols + rows),
            transcendentals=2 * rows * cols,
        ),
        name="last_score" if last else "score",
    )(*([order] if last else []), *parts, own, other, target, *earlier)


def finish_kernel(incoming, marks, scores):
    block = GROUPS
    for core in range(2):
        total = sum(
            jnp.sum(incoming[(x * 2 + core) * block : (x * 2 + core + 1) * block, :], axis=0, keepdims=True)
            for x in range(2)
        )
        half = total.shape[1] // 2
        group = half // 2
        result = total[:, half:] - jnp.log(total[:, :half])
        for t in range(2):
            row = slice(core * 2 + t, core * 2 + t + 1)
            part = result[:, t * group : (t + 1) * group]
            scores[row, :] = jnp.where(marks[row, :] > 0, part, 0.0)


def finish_scores(incoming, marks):
    near = pl.BlockSpec(memory_space=pltpu.VMEM)
    return pl.pallas_call(
        finish_kernel,
        in_specs=[near, near],
        out_specs=near,
        out_shape=jax.ShapeDtypeStruct(marks.shape, F32),
        compiler_params=pltpu.CompilerParams(vmem_limit_bytes=4 << 20),
        name="finish",
    )(incoming, marks)


def bring_kernel(source, target, sem):
    copy = pltpu.make_async_copy(source, target, sem)
    copy.start()
    copy.wait()


def bring_in(slice_of_head):
    return pl.pallas_call(
        bring_kernel,
        in_specs=[pl.BlockSpec(memory_space=pltpu.HBM)],
        out_specs=pl.BlockSpec(memory_space=pltpu.VMEM),
        scratch_shapes=[pltpu.SemaphoreType.DMA],
        out_shape=jax.ShapeDtypeStruct(slice_of_head.shape, slice_of_head.dtype),
        compiler_params=pltpu.CompilerParams(vmem_limit_bytes=8 << 20),
        cost_estimate=pl.CostEstimate(
            flops=0, bytes_accessed=2 * slice_of_head.size, transcendentals=0
        ),
        name="bring_in",
    )(slice_of_head)


def per_device(
    embedded,
    states,
    w_query,
    w_key,
    w_value,
    w_output_gate,
    w_beta,
    w_decay,
    decay_rate,
    decay_bias,
    head_gain,
    input_gain,
    w_out,
    final_gain,
    lm_head,
    targets,
    active,
):
    steps, group, width = embedded.shape
    me = lax.axis_index(AXES).astype(jnp.int32)
    core = lax.axis_index("c").astype(jnp.int32)
    batch = lax.axis_index(BATCH).astype(jnp.int32)
    send = functools.partial(lax.ppermute, axis_name=AXES)
    far_head = send(lm_head, perm=OTHER_CORE)

    give, keep = front(
        decay_rate,
        decay_bias,
        embedded,
        states,
        w_query,
        w_key,
        w_value,
        w_output_gate,
        w_beta.T,
        w_decay.T,
        w_out,
        input_gain[None],
        head_gain[None],
        active.T,
    )
    block = keep.shape[0]
    pair = (keep + send(give, perm=OTHER_CORE).astype(F32)).astype(BF16)
    pair, me, core, batch = lax.optimization_barrier((pair, me, core, batch))
    order = lax.dynamic_index_in_dim(jnp.asarray(sources()), me, 0, keepdims=False)
    wanted = lax.dynamic_slice_in_dim(targets.T, core * (steps // 2), steps // 2, 0)
    wanted = jnp.take(wanted.reshape(steps // 2, GROUPS, group), order, axis=1)
    wanted = wanted.transpose(1, 0, 2).reshape(1, GROUPS * block)
    marks = lax.dynamic_slice_in_dim(active.T, batch * group, group, 1)
    low, corner, high = [send(pair, perm=p) for p in (OTHER_LOW, OTHER_BOTH, OTHER_HIGH)]
    low, wanted, order, marks = lax.optimization_barrier((low, wanted, order, marks))

    def finish(a, b):
        y = a.astype(F32) + b.astype(F32)
        scale = lax.rsqrt(jnp.mean(y * y, axis=-1, keepdims=True) + EPS)
        return (y * scale * final_gain).astype(BF16)

    both = jnp.concatenate([finish(pair, low), finish(high, corner)], 0)
    far_head, both = lax.optimization_barrier((far_head, both))
    far_head = bring_in(far_head)
    ahead, behind, across = [send(both, perm=p) for p in NEAR]
    ahead, far_head = lax.optimization_barrier((ahead, far_head))
    one, two = jnp.concatenate([both, ahead], 0), jnp.concatenate([behind, across], 0)
    size = one.shape[0]
    forth_one, back_two = send(one, perm=FAR[0]), send(two, perm=FAR[1])
    forth_two, back_one = send(two, perm=FAR[0]), send(one, perm=FAR[1])
    own_head = lm_head
    halves = [send(forth_one, perm=FAR[0]), send(back_two, perm=FAR[1])]
    stats = []
    arrivals = ((one, two), (forth_one, back_two), (forth_two, back_one))
    for i, parts in enumerate(arrivals):
        stats.append(score(parts, own_head, far_head, wanted, 2 * size * i))
        wanted, stats[i] = lax.optimization_barrier((wanted, stats[i]))
    outgoing = score(halves, own_head, far_head, wanted, 6 * size, stats, order)
    incoming = lax.all_to_all(outgoing, AXES, 0, 0, tiled=True)
    return finish_scores(incoming, marks).T


def solution(mesh):
    finer = Mesh(mesh.devices.reshape(SIZES), AXES)
    return jax.shard_map(
        per_device,
        mesh=finer,
        in_specs=(
            P(None, BATCH, None),
            P(BATCH, HEAD, None, None),
            P(None, HEAD),
            P(None, HEAD),
            P(None, HEAD),
            P(None, HEAD),
            P(None, HEAD),
            P(None, HEAD),
            P(),
            P(),
            P(),
            P(),
            P(HEAD, None),
            P(),
            P(None, HEAD + BATCH),
            P(),
            P(),
        ),
        out_specs=P(BATCH, None),
        check_vma=False,
    )
```

```python
import functools

import jax
import jax.numpy as jnp
import numpy as np
from jax import lax
from jax.experimental import pallas as pl
from jax.experimental.pallas import tpu as pltpu
from jax.sharding import Mesh
from jax.sharding import PartitionSpec as P

DK = 128
DV = 128
EPS = 1e-06
AXES = ("xl", "c", "y", "z", "xh")
SIZES = (2, 2, 4, 4, 2)
HEAD = ("xl", "c")
BATCH = ("y", "z", "xh")
DEVICES = 128
GROUPS = 32
F32 = jnp.float32
BF16 = jnp.bfloat16


def route(move):
    pairs = []
    for source in range(DEVICES):
        spot = [int(i) for i in np.unravel_index(source, SIZES)]
        pairs.append((source, int(np.ravel_multi_index(move(*spot), SIZES))))
    return pairs


def shift(first, second, hops):
    def move(xl, c, y, z, xh):
        if (first, second)[c] == "y":
            return (xl, c, (y + hops) % 4, z, xh)
        return (xl, c, y, (z + hops) % 4, xh)

    return route(move)


OTHER_CORE = route(lambda xl, c, y, z, xh: (xl, 1 - c, y, z, xh))
OTHER_LOW = route(lambda xl, c, y, z, xh: (1 - xl, c, y, z, xh))
OTHER_HIGH = route(lambda xl, c, y, z, xh: (xl, c, y, z, 1 - xh))
OTHER_BOTH = route(lambda xl, c, y, z, xh: (1 - xl, c, y, z, 1 - xh))
NEAR = [shift("y", "z", k) for k in (1, 3, 2)]
FAR = [shift("z", "y", k) for k in (1, 3, 2)]


def sources():
    held = [[d % GROUPS] for d in range(DEVICES)]
    for stage in ([OTHER_HIGH], NEAR, FAR):
        grown = [list(h) for h in held]
        for pairs in stage:
            for source, target in pairs:
                grown[target].extend(held[source])
        held = grown
    landing = [*range(12), *range(20, 24), *range(12, 20), *range(24, 32)]
    return np.array(held, np.int32)[:, landing]


def position():
    xl, c, y, z, xh = [lax.axis_index(axis).astype(jnp.int32) for axis in AXES]
    return xl, c, xl * 2 + c, (y * 4 + z) * 2 + xh


def front_kernel(
    rate,
    offset,
    embedded,
    states,
    w_query,
    w_key,
    w_value,
    w_gate,
    w_beta,
    w_decay,
    w_out,
    input_gain,
    head_gain,
    active,
    give,
    keep,
    normed,
    kq,
    reads,
    beta_all,
    decay_all,
    marks,
    mixed,
    total,
):
    step = pl.program_id(0)
    steps, group, width = embedded.shape
    rows = steps * group
    low_x, core, head_group, batch_group = position()

    def contract_last(a, b):
        return lax.dot_general(a, b, (((1,), (1,)), ((), ())), preferred_element_type=F32)

    @pl.when(step == 0)
    def _():
        for t in range(steps):
            e = embedded[t].astype(F32)
            scale = lax.rsqrt(jnp.mean(e * e, axis=-1, keepdims=True) + EPS)
            normed[t * group : (t + 1) * group, :] = (e * scale * input_gain[...]).astype(BF16)
        n = normed[...]
        beta_raw = contract_last(n, w_beta[...]).astype(BF16).astype(F32)
        decay_raw = contract_last(n, w_decay[...]).astype(BF16).astype(F32)
        for h in range(w_beta.shape[0]):
            b = jnp.broadcast_to(beta_raw[:, h : h + 1], (rows, DV))
            d = jnp.broadcast_to(decay_raw[:, h : h + 1], (rows, DV))
            at = head_group * w_beta.shape[0] + h
            beta_all[h] = jax.nn.sigmoid(b)
            decay_all[h] = jnp.exp(-rate[at] * jax.nn.softplus(d + offset[at]))
        requests = active.shape[1]
        here = lax.broadcasted_iota(jnp.int32, (group, requests), 1) == (
            batch_group * group + lax.broadcasted_iota(jnp.int32, (group, requests), 0)
        )
        for t in range(steps):
            line = jnp.broadcast_to(active[t : t + 1, :].astype(F32), (group, requests))
            column = jnp.sum(jnp.where(here, line, 0.0), axis=1, keepdims=True)
            marks[t] = jnp.broadcast_to(column, (group, DV))

    n = normed[...]

    def project(weight):
        return jnp.dot(n, weight[...], preferred_element_type=F32).astype(BF16).astype(F32)

    def unit(x):
        return x * lax.rsqrt(jnp.sum(x * x, axis=-1, keepdims=True) + EPS)

    kq[:rows, :] = unit(project(w_key))
    kq[rows:, :] = unit(project(w_query)) * DK ** (-0.5)
    value = project(w_value)
    gate = project(w_gate)
    k = [kq[t * group : (t + 1) * group, :] for t in range(steps)]
    q = [kq[rows + t * group : rows + (t + 1) * group, :] for t in range(steps)]

    def inner(a, b):
        return jnp.broadcast_to(jnp.sum(a * b, axis=-1, keepdims=True), (group, DV))

    kk = {(t, i): inner(k[t], k[i]) for t in range(steps) for i in range(t)}
    qk = {(t, i): inner(q[t], k[i]) for t in range(steps) for i in range(t + 1)}
    for r in range(group):
        lines = kq[pl.ds(r, 2 * steps, stride=group), :]
        high = lines.astype(BF16).astype(F32)
        both = jnp.concatenate([high, lines - high], axis=0).astype(BF16)
        for h in range(2):
            got = jnp.dot(both, states[r, h], preferred_element_type=F32)
            reads[h, pl.ds(r, 2 * steps, stride=group), :] = got[: 2 * steps] + got[2 * steps :]
    for h in range(2):
        head = 2 * step + h
        coefficient = []
        update = []
        for t in range(steps):
            at = slice(t * group, (t + 1) * group)
            decay = decay_all[head, at, :]
            beta = beta_all[head, at, :]
            mark = marks[t] > 0
            of_key = reads[h, at, :]
            of_query = reads[h, rows + t * group : rows + (t + 1) * group, :]
            if t > 0:
                of_key = start * of_key
                of_query = start * of_query
            for i in range(t):
                of_key = of_key + coefficient[i] * kk[t, i] * update[i]
                of_query = of_query + coefficient[i] * qk[t, i] * update[i]
            u = beta * (value[at, h * DV : (h + 1) * DV] - decay * of_key)
            readout = decay * of_query + qk[t, t] * u
            faded = jnp.where(mark, decay, 1.0)
            start = faded if t == 0 else start * faded
            coefficient = [old * faded for old in coefficient] + [jnp.where(mark, 1.0, 0.0)]
            update.append(u)
            scale = lax.rsqrt(jnp.mean(readout * readout, axis=-1, keepdims=True) + EPS)
            g = gate[at, h * DV : (h + 1) * DV]
            mixed[at, h * DV : (h + 1) * DV] = (
                readout * scale * head_gain[...] * (g * jax.nn.sigmoid(g))
            ).astype(BF16)
    part = jnp.dot(mixed[...], w_out[...], preferred_element_type=F32)

    @pl.when(step == 0)
    def _():
        total[...] = part

    @pl.when(step > 0)
    def _():
        total[...] += part

    @pl.when(step == pl.num_programs(0) - 1)
    def _():
        half = rows // 2
        c = core
        tokens = embedded[pl.ds(c * (steps // 2), steps // 2)].astype(F32).reshape(half, width)
        first = jnp.where(low_x == 0, 1.0, 0.0)
        keep[...] = total[pl.ds(pl.multiple_of(c * half, half), half), :] + tokens * first
        give[...] = total[pl.ds(pl.multiple_of((1 - c) * half, half), half), :].astype(BF16)


def front(rate, offset, embedded, states, wq, wk, wv, wg, wb, wd, wo, ig, hg, active):
    steps, group, width = embedded.shape
    rows, heads = steps * group, states.shape[1]
    key_heads = heads // 2
    whole = lambda *shape: pl.BlockSpec(shape, lambda j, *_: (0,) * len(shape))
    across = lambda cols: pl.BlockSpec((width, cols), lambda j, *_: (0, j))
    return pl.pallas_call(
        front_kernel,
        grid_spec=pltpu.PrefetchScalarGridSpec(
            num_scalar_prefetch=2,
            grid=(key_heads,),
            in_specs=[
                whole(steps, group, width),
                pl.BlockSpec((group, 2, DK, DV), lambda j, *_: (0, j, 0, 0)),
                across(DK),
                across(DK),
                across(2 * DV),
                across(2 * DV),
                whole(heads, width),
                whole(heads, width),
                pl.BlockSpec((2 * DV, width), lambda j, *_: (j, 0)),
                whole(1, width),
                whole(1, DV),
                whole(*active.shape),
            ],
            out_specs=[whole(rows // 2, width), whole(rows // 2, width)],
            scratch_shapes=[
                pltpu.VMEM((rows, width), BF16),
                pltpu.VMEM((2 * rows, DK), F32),
                pltpu.VMEM((2, 2 * rows, DV), F32),
                pltpu.VMEM((heads, rows, DV), F32),
                pltpu.VMEM((heads, rows, DV), F32),
                pltpu.VMEM((steps, group, DV), F32),
                pltpu.VMEM((rows, 2 * DV), BF16),
                pltpu.VMEM((rows, width), F32),
            ],
        ),
        out_shape=[
            jax.ShapeDtypeStruct((rows // 2, width), BF16),
            jax.ShapeDtypeStruct((rows // 2, width), F32),
        ],
        compiler_params=pltpu.CompilerParams(
            dimension_semantics=("arbitrary",), vmem_limit_bytes=60 << 20
        ),
        cost_estimate=pl.CostEstimate(
            flops=2 * rows * width * 4096, bytes_accessed=21 << 20, transcendentals=0
        ),
        name="front",
    )(rate, offset, embedded, states, wq, wk, wv, wg, wb, wd, wo, ig, hg, active)


TILE = 512


def score_block(parts, own, other, target, offset):
    piece = jnp.concatenate([part[...] for part in parts], axis=0)
    size, cols = piece.shape[0], own.shape[1]
    _, core, head_group, batch_group = position()
    base = (head_group * GROUPS + batch_group) * cols
    bases = (base, base + (1 - 2 * core) * GROUPS * cols)
    lane = lax.broadcasted_iota(jnp.int32, (size, 128), 1)
    want = jnp.broadcast_to(target[:, offset : offset + size], (128, size)).T - lane
    running = jnp.zeros((size, 128), F32)
    found = jnp.zeros((size, 128), F32)
    for start in range(0, cols, TILE):
        for base, weight in zip(bases, (own, other)):
            logits = jnp.dot(piece, weight[:, start : start + TILE], preferred_element_type=F32)
            left = want - (base + start)
            for s in range(0, TILE, 128):
                part = logits[:, s : s + 128]
                running = running + jnp.exp(part)
                found = found + jnp.where(left == s, part, 0.0)
    sums = jnp.sum(running, axis=1, keepdims=True)
    hits = jnp.sum(found, axis=1, keepdims=True)
    return jnp.where(lane == 0, sums, hits).T[:8, :]


def score_kernel(offset, one, two, own, other, target, stats):
    stats[...] = score_block((one, two), own, other, target, offset)


def rows_score_kernel(offset, begun, order, one, two, own, other, target, *refs):
    earlier, outgoing = refs[:-1], refs[-1]
    mine = score_block((one, two), own, other, target, offset)
    if begun:
        outgoing[...] = earlier[0][...]
        blocks = [mine]
    else:
        outgoing[...] = jnp.zeros_like(outgoing)
        blocks = [*(part[...] for part in earlier), mine]
    half = outgoing.shape[1] // 2
    at = begun
    for block in blocks:
        for s in range(0, block.shape[1], half):
            row = jnp.concatenate([block[0:1, s : s + half], block[1:2, s : s + half]], axis=1)
            for head in range(4):
                outgoing[pl.ds(order[at] + head * GROUPS, 1), :] = row
            at += 1


def score(parts, own, other, target, offset, earlier=(), order=None, begun=0):
    size, width = parts[0].shape
    rows, cols = 2 * size, own.shape[1]
    near = pl.BlockSpec(memory_space=pltpu.VMEM)
    last = order is not None
    kernel = functools.partial(score_kernel, offset)
    if last:
        kernel = functools.partial(rows_score_kernel, offset, begun)
    shape = (DEVICES, 2 * rows * 4 // GROUPS) if last else (8, rows)
    return pl.pallas_call(
        kernel,
        grid_spec=pltpu.PrefetchScalarGridSpec(
            num_scalar_prefetch=int(last),
            grid=(),
            in_specs=[near] * (5 + len(earlier)),
            out_specs=near,
        ),
        out_shape=jax.ShapeDtypeStruct(shape, F32),
        compiler_params=pltpu.CompilerParams(vmem_limit_bytes=20 << 20),
        cost_estimate=pl.CostEstimate(
            flops=4 * rows * width * cols,
            bytes_accessed=2 * width * (2 * cols + rows),
            transcendentals=2 * rows * cols,
        ),
        name="rows_score" if last else "score",
    )(*([order] if last else []), *parts, own, other, target, *earlier)


def finish_kernel(incoming, marks, scores):
    block = GROUPS
    for core in range(2):
        total = sum(
            jnp.sum(incoming[(x * 2 + core) * block : (x * 2 + core + 1) * block, :], axis=0, keepdims=True)
            for x in range(2)
        )
        half = total.shape[1] // 2
        group = half // 2
        result = total[:, half:] - jnp.log(total[:, :half])
        for t in range(2):
            row = slice(core * 2 + t, core * 2 + t + 1)
            part = result[:, t * group : (t + 1) * group]
            scores[row, :] = jnp.where(marks[row, :] > 0, part, 0.0)


def finish_scores(incoming, marks):
    near = pl.BlockSpec(memory_space=pltpu.VMEM)
    return pl.pallas_call(
        finish_kernel,
        in_specs=[near, near],
        out_specs=near,
        out_shape=jax.ShapeDtypeStruct(marks.shape, F32),
        compiler_params=pltpu.CompilerParams(vmem_limit_bytes=4 << 20),
        name="finish",
    )(incoming, marks)


def bring_kernel(source, target, sem):
    copy = pltpu.make_async_copy(source, target, sem)
    copy.start()
    copy.wait()


def bring_in(slice_of_head):
    return pl.pallas_call(
        bring_kernel,
        in_specs=[pl.BlockSpec(memory_space=pltpu.HBM)],
        out_specs=pl.BlockSpec(memory_space=pltpu.VMEM),
        scratch_shapes=[pltpu.SemaphoreType.DMA],
        out_shape=jax.ShapeDtypeStruct(slice_of_head.shape, slice_of_head.dtype),
        compiler_params=pltpu.CompilerParams(vmem_limit_bytes=8 << 20),
        cost_estimate=pl.CostEstimate(
            flops=0, bytes_accessed=2 * slice_of_head.size, transcendentals=0
        ),
        name="bring_in",
    )(slice_of_head)


def per_device(
    embedded,
    states,
    w_query,
    w_key,
    w_value,
    w_output_gate,
    w_beta,
    w_decay,
    decay_rate,
    decay_bias,
    head_gain,
    input_gain,
    w_out,
    final_gain,
    lm_head,
    targets,
    active,
):
    steps, group, width = embedded.shape
    me = lax.axis_index(AXES).astype(jnp.int32)
    core = lax.axis_index("c").astype(jnp.int32)
    batch = lax.axis_index(BATCH).astype(jnp.int32)
    send = functools.partial(lax.ppermute, axis_name=AXES)
    far_head = send(lm_head, perm=OTHER_CORE)

    give, keep = front(
        decay_rate,
        decay_bias,
        embedded,
        states,
        w_query,
        w_key,
        w_value,
        w_output_gate,
        w_beta.T,
        w_decay.T,
        w_out,
        input_gain[None],
        head_gain[None],
        active.T,
    )
    block = keep.shape[0]
    pair = (keep + send(give, perm=OTHER_CORE).astype(F32)).astype(BF16)
    pair, me, core, batch = lax.optimization_barrier((pair, me, core, batch))
    order = lax.dynamic_index_in_dim(jnp.asarray(sources()), me, 0, keepdims=False)
    wanted = lax.dynamic_slice_in_dim(targets.T, core * (steps // 2), steps // 2, 0)
    wanted = jnp.take(wanted.reshape(steps // 2, GROUPS, group), order, axis=1)
    wanted = wanted.transpose(1, 0, 2).reshape(1, GROUPS * block)
    marks = lax.dynamic_slice_in_dim(active.T, batch * group, group, 1)
    low, corner, high = [send(pair, perm=p) for p in (OTHER_LOW, OTHER_BOTH, OTHER_HIGH)]
    low, wanted, order, marks = lax.optimization_barrier((low, wanted, order, marks))

    def finish(a, b):
        y = a.astype(F32) + b.astype(F32)
        scale = lax.rsqrt(jnp.mean(y * y, axis=-1, keepdims=True) + EPS)
        return (y * scale * final_gain).astype(BF16)

    both = jnp.concatenate([finish(pair, low), finish(high, corner)], 0)
    far_head, both = lax.optimization_barrier((far_head, both))
    far_head = bring_in(far_head)
    ahead, behind, across = [send(both, perm=p) for p in NEAR]
    ahead, far_head = lax.optimization_barrier((ahead, far_head))
    one, two = jnp.concatenate([both, ahead], 0), jnp.concatenate([behind, across], 0)
    size = one.shape[0]
    forth_one, back_two = send(one, perm=FAR[0]), send(two, perm=FAR[1])
    forth_two, back_one = send(two, perm=FAR[0]), send(one, perm=FAR[1])
    own_head = lm_head
    halves = [send(forth_one, perm=FAR[0]), send(back_two, perm=FAR[1])]
    near = score((one, two), own_head, far_head, wanted, 0)
    wanted, near = lax.optimization_barrier((wanted, near))
    side = score((forth_one, back_two), own_head, far_head, wanted, 2 * size)
    wanted, side = lax.optimization_barrier((wanted, side))
    outgoing = score(
        (forth_two, back_one), own_head, far_head, wanted, 4 * size, (near, side), order
    )
    begun = 3 * (2 * size // block)
    outgoing = score(
        halves, own_head, far_head, wanted, 6 * size, (outgoing,), order, begun
    )
    incoming = lax.all_to_all(outgoing, AXES, 0, 0, tiled=True)
    return finish_scores(incoming, marks).T


def solution(mesh):
    finer = Mesh(mesh.devices.reshape(SIZES), AXES)
    return jax.shard_map(
        per_device,
        mesh=finer,
        in_specs=(
            P(None, BATCH, None),
            P(BATCH, HEAD, None, None),
            P(None, HEAD),
            P(None, HEAD),
            P(None, HEAD),
            P(None, HEAD),
            P(None, HEAD),
            P(None, HEAD),
            P(),
            P(),
            P(),
            P(),
            P(HEAD, None),
            P(),
            P(None, HEAD + BATCH),
            P(),
            P(),
        ),
        out_specs=P(BATCH, None),
        check_vma=False,
    )
```
